32 devices in a mesh: dp: 4 (over x, core), fsdp: 8 (over z, y).
Axes of the slice: x: 2, y: 2, z: 4, core: 2. Of those that a mesh axis runs over, the one named last changes fastest.
Arguments:
- token_ids: int32 [4096], P('dp'), may hold values from 0 to 15263, as said below
- embed_table: bfloat16 [15264, 768], P('fsdp'), may hold values from -16 to 16, as said below
- w_qkv: bfloat16 [768, 2304], P('fsdp'), may hold values from -2 to 2
- w_out: bfloat16 [768, 768], P('fsdp'), may hold values from -0.21875 to 0.21875
- ln_gain: float32 [768], replicated, may hold values from 0.5 to 1.5
- ln_bias: float32 [768], replicated, may hold values from -1 to 1
- centroids_t: bfloat16 [768, 32768], P('fsdp', 'dp'), may hold values from -24 to 24
- assignments: int32 [4096], replicated, may hold values from 0 to 32767, as said below
Outputs:
- token_loss: float32 [4096], P(('dp', 'fsdp'))
- new_centroids: float32 [32768, 768], P(('dp', 'fsdp'))
The draws below stay inside these ranges and needn't reach their ends.
Inputs may be any that keep to these rules, and one draw needn't show every extreme that they name: `token_ids`: id 0 is padding; a passage may end in a run of padding. `embed_table`: token embeddings of order one. `assignments`: cluster sizes are skewed.
All inputs are finite; a program needn't handle non-finite values.
Results may differ from the reference program's by a relative error of at most 0.0055.
Values may be sent and summed in bfloat16 or wider, within the bound.
A program may use at most 64 MiB of HBM per device.

```python
import math
import jax
import jax.numpy as jnp
from jax import lax

D = 768
HEADS = 12
HEAD = 64
VOCAB = 15264
SEQ = 128
CENT = 32768
TOKENS = 4096


def shared_bias(key):
    spread = 0.1
    return spread * jax.random.normal(jax.random.fold_in(key, 7), (D,), jnp.float32)


def skewed_ranks(key, count, limit):
    levels = (limit - 1).bit_length()
    level = jax.random.randint(jax.random.fold_in(key, 1), (count,), 0, levels + 1).astype(jnp.int32)
    upper = jnp.minimum(jnp.left_shift(jnp.ones((count,), jnp.int32), level), limit).astype(jnp.int32)
    return jax.random.randint(jax.random.fold_in(key, 2), (count,), 0, upper).astype(jnp.int32)


def draw_token_ids(key, part):
    passages = TOKENS // SEQ
    ranks = skewed_ranks(jax.random.fold_in(key, 31), TOKENS, VOCAB - 1)
    order = jax.random.permutation(jax.random.fold_in(key, 32), VOCAB - 1).astype(jnp.int32)
    words = order[ranks] + 1
    lengths = jax.random.randint(jax.random.fold_in(key, 33), (passages, 1), SEQ // 8, SEQ + 1).astype(jnp.int32)
    positions = jnp.arange(SEQ, dtype=jnp.int32)
    padded = positions[None, :] >= lengths
    words = jnp.where(padded, jnp.zeros_like(words.reshape(passages, SEQ)), words.reshape(passages, SEQ))
    return words.reshape(TOKENS).astype(jnp.int32)


def draw_assignments(key, part):
    ranks = skewed_ranks(jax.random.fold_in(key, 41), TOKENS, CENT)
    order = jax.random.permutation(jax.random.fold_in(key, 42), CENT).astype(jnp.int32)
    spread_part = order[ranks]
    span = CENT // 8
    first = jax.random.randint(jax.random.fold_in(key, 43), (), 0, 8).astype(jnp.int32) * span
    crowded = first + jax.random.randint(jax.random.fold_in(key, 44), (TOKENS,), 0, span).astype(jnp.int32)
    chosen = jax.random.permutation(jax.random.fold_in(key, 45), TOKENS).astype(jnp.int32) < TOKENS // 4
    return jnp.where(chosen, crowded, spread_part).astype(jnp.int32)


def draw_ln_bias(key, part):
    return shared_bias(key).astype(jnp.float32)


def draw_embed_table(key, part):
    values = jax.random.normal(jax.random.fold_in(key, 3), (VOCAB, D), jnp.float32)
    values = jnp.clip(values, -5.0, 5.0)
    return values.astype(jnp.bfloat16)


def draw_w_qkv(key, part):
    factor = 1.0 / jnp.sqrt(jnp.float32(D))
    parts = jnp.clip(jax.random.normal(jax.random.fold_in(key, 5), (D, 3 * D), jnp.float32), -5.0, 5.0) * factor
    return parts.astype(jnp.bfloat16)


def draw_centroids_t(key, part):
    values = 0.1 * jnp.clip(jax.random.normal(jax.random.fold_in(key, 11), (D, CENT), jnp.float32), -5.0, 5.0)
    return values.astype(jnp.bfloat16)


def block_levels(stream_key, dims, cuts, smallest, top_value):
    def one(axis_at, shards_of):
        heights = jax.random.uniform(jax.random.fold_in(jax.random.fold_in(stream_key, 6), axis_at), (shards_of,), jnp.float32, smallest / len(cuts), top_value / len(cuts))
        return jnp.repeat(jnp.exp(heights), dims[axis_at] // shards_of).reshape((-1,) + (1,) * (len(dims) - axis_at - 1))

    factor_of = one(*cuts[0])
    for cut in cuts[1:]:
        factor_of = factor_of * one(*cut)
    return factor_of


def centred(key, extent, deviation, most, cuts=(), kind=jnp.bfloat16):
    values = jax.random.normal(key, extent, jnp.float32) * deviation
    if len(cuts) > 0:
        values = block_levels(key, extent, cuts, -0.22, 0.18) * values
    return jnp.clip(values, min=-most, max=most).astype(kind)


def setup_inputs(seed: int = 0) -> dict:
    key_of = jax.random.split(jax.random.key(seed), 9)
    token_ids = draw_token_ids(jax.random.fold_in(key_of[8], 71), 0)
    embed_table = draw_embed_table(jax.random.fold_in(key_of[8], 71), 0)
    w_qkv = draw_w_qkv(jax.random.fold_in(key_of[8], 71), 0)
    w_out = centred(key_of[3], (D, D), D ** -0.5, 0.21875, ((0, 8),))
    ln_gain = jnp.clip(1.0 + 0.1 * jax.random.normal(key_of[4], (D,), jnp.float32), 0.5, 1.5)
    ln_bias = draw_ln_bias(jax.random.fold_in(key_of[8], 71), 0)
    centroids_t = draw_centroids_t(jax.random.fold_in(key_of[8], 71), 0)
    assignments = draw_assignments(jax.random.fold_in(key_of[8], 71), 0)
    return dict(token_ids=token_ids, embed_table=embed_table, w_qkv=w_qkv, w_out=w_out, ln_gain=ln_gain, ln_bias=ln_bias, centroids_t=centroids_t, assignments=assignments)


def layer_norm(values, ln_gain, ln_bias):
    center = values - lax.optimization_barrier(jnp.mean(values, axis=-1, keepdims=True))
    spread = lax.optimization_barrier(jnp.mean(center * center, axis=-1, keepdims=True))
    return center * lax.rsqrt(spread + 1e-05) * ln_gain + ln_bias

def reference(token_ids, embed_table, w_qkv, w_out, ln_gain, ln_bias, centroids_t, assignments):
    inputs = embed_table[token_ids]
    passages = TOKENS // SEQ
    packed = jnp.dot(inputs, w_qkv, preferred_element_type=jnp.float32).astype(jnp.bfloat16)
    packed = packed.reshape(passages, SEQ, 3, HEADS, HEAD).astype(jnp.float32)
    scores = jnp.einsum('bqhd,bkhd->bhqk', packed[:, :, 0], packed[:, :, 1]) * (1.0 / math.sqrt(HEAD))
    probs = jax.nn.softmax(scores, axis=-1).astype(jnp.bfloat16)
    context = jnp.einsum('bhqk,bkhd->bqhd', probs.astype(jnp.float32), packed[:, :, 2])
    context = context.astype(jnp.bfloat16).reshape(TOKENS, D)
    mixed = jnp.dot(context, w_out, preferred_element_type=jnp.float32) + inputs.astype(jnp.float32)
    embedded = layer_norm(mixed, ln_gain, ln_bias).astype(jnp.bfloat16)
    block = math.gcd(TOKENS, 512)

    def score_rows(pieces):
        rows, assigned = pieces
        logits = jnp.dot(rows, centroids_t, preferred_element_type=jnp.float32)
        peak = lax.optimization_barrier(jnp.max(logits, axis=1))
        total = jnp.log(lax.optimization_barrier(jnp.sum(jnp.exp(logits - peak[:, None]), axis=1))) + peak
        chosen = jnp.take_along_axis(logits, assigned[:, None], axis=1)[:, 0]
        return total - chosen
    token_loss = lax.map(score_rows, (embedded.reshape(TOKENS // block, block, D), assignments.reshape(TOKENS // block, block))).reshape(TOKENS)
    sums = jax.ops.segment_sum(embedded.astype(jnp.float32), assignments, num_segments=CENT)
    counts = jax.ops.segment_sum(jnp.ones((TOKENS,), jnp.int32), assignments, num_segments=CENT)
    previous = centroids_t.T.astype(jnp.float32)
    new_centroids = jnp.where(counts[:, None] > 0, sums / jnp.maximum(counts, 1)[:, None].astype(jnp.float32), previous)
    return (token_loss, new_centroids)
```

```python
import functools
import math

import jax
import jax.numpy as jnp
from jax import lax
from jax.experimental import pallas as pl
from jax.experimental.pallas import tpu as pltpu
from jax.sharding import PartitionSpec as P

HEADS = 12
HEAD = 64
SEQ = 128


def joined(shard, axis, combine):
    everything = jax.tree.map(lambda part: lax.all_gather(part, axis), shard)
    initial = jax.tree.map(lambda part: part[0], everything)

    def lap(k, so_far):
        return combine(so_far, jax.tree.map(lambda part: part[k], everything))

    return lax.fori_loop(1, lax.axis_size(axis), lap, initial)


def layer_norm(values, ln_gain, ln_bias):
    center = values - jnp.mean(values, axis=-1, keepdims=True)
    spread = jnp.mean(center * center, axis=-1, keepdims=True)
    return center * lax.rsqrt(spread + 1e-05) * ln_gain + ln_bias


def encode(inputs, qkv_full, out_full, ln_gain, ln_bias):
    passages = inputs.shape[0] // SEQ
    packed = jnp.dot(inputs, qkv_full, preferred_element_type=jnp.float32).astype(jnp.bfloat16)
    packed = packed.reshape(passages, SEQ, 3, HEADS, HEAD)
    scores = jnp.einsum(
        "bqhd,bkhd->bhqk", packed[:, :, 0], packed[:, :, 1], preferred_element_type=jnp.float32
    ) * (1.0 / math.sqrt(HEAD))
    probs = jax.nn.softmax(scores, axis=-1).astype(jnp.bfloat16)
    context = jnp.einsum(
        "bhqk,bkhd->bqhd", probs, packed[:, :, 2], preferred_element_type=jnp.float32
    )
    context = context.astype(jnp.bfloat16).reshape(inputs.shape[0], HEADS * HEAD)
    mixed = jnp.dot(context, out_full, preferred_element_type=jnp.float32) + inputs.astype(
        jnp.float32
    )
    return layer_norm(mixed, ln_gain, ln_bias).astype(jnp.bfloat16)


def one_hot_sums(rows, targets, width):
    count = rows.shape[0]
    step_rows = math.gcd(count, 512)
    columns = jnp.arange(width, dtype=jnp.int32)

    def one_visit(totals, pieces):
        block_rows, block_targets = pieces
        hits = (block_targets[:, None] == columns[None, :]).astype(jnp.bfloat16)
        return (
            totals
            + lax.dot_general(
                hits, block_rows, (((0,), (0,)), ((), ())), preferred_element_type=jnp.float32
            ),
            None,
        )

    start = jnp.zeros((width, rows.shape[1]), jnp.float32)
    totals, unused = lax.scan(
        one_visit,
        start,
        (
            rows.reshape(count // step_rows, step_rows, rows.shape[1]),
            targets.reshape(count // step_rows, step_rows),
        ),
    )
    return totals


def combine_parts(first, second):
    peak = jnp.maximum(first[0], second[0])
    mass = first[1] * jnp.exp(first[0] - peak) + second[1] * jnp.exp(second[0] - peak)
    return (peak, mass, first[2] + second[2])


def shards(token_ids, embed_table, w_qkv, w_out, ln_gain, ln_bias, centroids_t, assignments):
    dp_size = lax.axis_size("dp")
    fsdp_size = lax.axis_size("fsdp")
    dp_rank = lax.axis_index("dp")
    fsdp_rank = lax.axis_index("fsdp")
    vocab_rows = embed_table.shape[0]
    local_ids = token_ids - fsdp_rank * vocab_rows
    inside = (local_ids >= 0) & (local_ids < vocab_rows)
    looked = jnp.take(embed_table, jnp.clip(local_ids, 0, vocab_rows - 1), axis=0)
    looked = jnp.where(inside[:, None], looked, jnp.zeros_like(looked))
    inputs = (
        lax.psum_scatter(looked, "fsdp", scatter_dimension=0, tiled=True)
        .astype(jnp.float32)
        .astype(jnp.bfloat16)
    )
    qkv_full, out_full, cent_full = (
        lax.all_gather(w_qkv, "fsdp", axis=0, tiled=True),
        lax.all_gather(w_out, "fsdp", axis=0, tiled=True),
        lax.all_gather(centroids_t, "fsdp", axis=0, tiled=True),
    )
    encoded = encode(inputs, qkv_full, out_full, ln_gain, ln_bias)
    own_rows = encoded.shape[0]
    width = encoded.shape[1]
    block_width = cent_full.shape[1]
    per_dev = block_width // fsdp_size
    slab = lax.all_gather(encoded, "dp", axis=0, tiled=True)
    slab_assign = lax.dynamic_index_in_dim(
        assignments.reshape(dp_size, fsdp_size, own_rows), fsdp_rank, 1, keepdims=False
    ).reshape(-1)
    owned = slab_assign - dp_rank * block_width
    slab_rows = slab.shape[0]
    step_rows = math.gcd(slab_rows, 512)
    columns = jnp.arange(block_width, dtype=jnp.int32)

    def body_visit(totals, pieces):
        block_rows, local = pieces
        logits = jnp.dot(block_rows, cent_full, preferred_element_type=jnp.float32)
        peak = jnp.max(logits, axis=1)
        mass = jnp.sum(jnp.exp(logits - peak[:, None]), axis=1)
        hits = local[:, None] == columns[None, :]
        picked = jnp.sum(jnp.where(hits, logits, 0.0), axis=1)
        return (totals, (peak, mass, picked))

    start = jnp.zeros((1,), jnp.float32)
    partial_value, stats = lax.scan(
        body_visit,
        start,
        (
            slab.reshape(slab_rows // step_rows, step_rows, width),
            owned.reshape(slab_rows // step_rows, step_rows),
        ),
    )
    peaks, masses, picks = (stats[0].reshape(-1), stats[1].reshape(-1), stats[2].reshape(-1))
    peaks, masses, picks = joined((peaks, masses, picks), "dp", combine_parts)
    peak_own = lax.dynamic_slice_in_dim(peaks, dp_rank * own_rows, own_rows)
    mass_own = lax.dynamic_slice_in_dim(masses, dp_rank * own_rows, own_rows)
    pick_own = lax.dynamic_slice_in_dim(picks, dp_rank * own_rows, own_rows)
    token_loss = jnp.log(mass_own) + peak_own - pick_own
    share = lax.all_to_all(encoded, "fsdp", split_axis=1, concat_axis=0, tiled=True)
    every_rows = lax.all_gather(share, "dp", axis=0, tiled=True)
    block_local = assignments - dp_rank * block_width
    partial_share = one_hot_sums(every_rows, block_local, block_width)
    totals = lax.all_to_all(partial_share, "fsdp", split_axis=0, concat_axis=1, tiled=True)
    base = dp_rank * block_width + fsdp_rank * per_dev
    targets = base + jnp.arange(per_dev, dtype=jnp.int32)
    counts = jnp.sum((assignments[:, None] == targets[None, :]).astype(jnp.int32), axis=0)
    previous = lax.dynamic_slice_in_dim(cent_full, fsdp_rank * per_dev, per_dev, 1).T.astype(
        jnp.float32
    )
    new_centroids = jnp.where(
        counts[:, None] > 0, totals / jnp.maximum(counts, 1)[:, None].astype(jnp.float32), previous
    )
    return (token_loss, new_centroids)


VMEM_LIMIT = 46 * 1024 * 1024
CUTS = 2
WHOLE_VMEM = pl.BlockSpec(memory_space=pltpu.VMEM)


class Place:
    def __init__(self, deep):
        self.deep = deep
        self.dp, self.fsdp = lax.axis_index("dp"), lax.axis_index("fsdp")
        self.x, self.c = self.dp // 2, self.dp % 2
        self.z, self.y = self.fsdp // 2, self.fsdp % 2

    def at(self, x=None, c=None, z=None, y=None):
        x, c = self.x if x is None else x, self.c if c is None else c
        z, y = self.z if z is None else z, self.y if y is None else y
        return {"dp": x * 2 + c, "fsdp": z * 2 + y}

    def greet(self):
        barrier = pltpu.get_barrier_semaphore()
        everyone = 8 * self.deep
        me = self.dp * 2 * self.deep + self.fsdp

        @pl.loop(1, everyone)
        def each(k):
            peer = (me + k) % everyone
            there = {"dp": peer // (2 * self.deep), "fsdp": peer % (2 * self.deep)}
            pl.semaphore_signal(barrier, inc=1, device_id=there, device_id_type=pl.DeviceIdType.MESH)

    def met(self):
        pl.semaphore_wait(pltpu.get_barrier_semaphore(), 8 * self.deep - 1)


class Sender:
    def __init__(self, sems):
        self.sems, self.used, self.sent = sems, 0, []

    def send(self, src, dst, recv_sem, peer, when=None):
        copy = pltpu.make_async_remote_copy(
            src_ref=src,
            dst_ref=dst,
            send_sem=self.sems.at[self.used],
            recv_sem=recv_sem,
            device_id=peer,
            device_id_type=pl.DeviceIdType.MESH,
        )
        self.used += 1
        self.sent.append((copy, when))
        guarded(when, copy.start)

    def arrived(self, dst, recv_sem, peer, when=None):
        copy = pltpu.make_async_remote_copy(
            src_ref=dst,
            dst_ref=dst,
            send_sem=self.sems.at[0],
            recv_sem=recv_sem,
            device_id=peer,
            device_id_type=pl.DeviceIdType.MESH,
        )
        guarded(when, copy.wait_recv)

    def drain(self):
        for copy, when in self.sent:
            guarded(when, copy.wait_send)


def guarded(when, action):
    if when is None:
        action()
    else:
        pl.when(when)(action)


def near_first(z, k, deep):
    below, above = z, deep - 1 - z
    both = jnp.minimum(below, above)
    swing = z - (k + 1) // 2 if k % 2 else z + k // 2
    far = jnp.where(above > below, z + k - both, z - k + both)
    return jnp.where(k <= 2 * both, swing, far)


def passage(x, quarters, gain, bias, w_ref):
    width = x.shape[1]

    def dense(rows, q):
        weights = w_ref[q].reshape(width, width)
        return jnp.dot(rows, weights, preferred_element_type=jnp.float32)

    query, key, value = (dense(x, q).astype(jnp.bfloat16) for q in quarters[:3])
    context = []
    for head in range(HEADS):
        at = slice(head * HEAD, (head + 1) * HEAD)
        scores = lax.dot_general(
            query[:, at], key[:, at], (((1,), (1,)), ((), ())), preferred_element_type=jnp.float32
        ) * (1.0 / math.sqrt(HEAD))
        weight = jnp.exp(scores - jnp.max(scores, axis=1, keepdims=True))
        probs = (weight / jnp.sum(weight, axis=1, keepdims=True)).astype(jnp.bfloat16)
        context.append(jnp.dot(probs, value[:, at], preferred_element_type=jnp.float32))
    context = jnp.concatenate(context, axis=1).astype(jnp.bfloat16)
    mixed = dense(context, quarters[3]) + x.astype(jnp.float32)
    return layer_norm(mixed, gain, bias).astype(jnp.bfloat16)


def step_kernel(
    deep,
    ids_hbm,
    table_hbm,
    qkv_hbm,
    out_w_hbm,
    gain_hbm,
    bias_hbm,
    cent_hbm,
    assign_hbm,
    loss_ref,
    new_ref,
    ids,
    table,
    gain,
    bias,
    assign,
    id_columns,
    rows,
    w,
    from_y,
    joined_y,
    from_mate,
    from_far,
    cent,
    old,
    mine,
    tokens,
    hot,
    counts,
    stat,
    got,
    load_sems,
    send_sems,
    y_sems,
    mate_sems,
    far_sems,
    w_sems,
    cent_sems,
    token_sems,
    stat_send,
    stat_recv,
):
    place = Place(deep)
    x, c, z, y = place.x, place.c, place.z, place.y
    own = place.fsdp
    parts = 2 * deep
    vocab_rows, width = table.shape
    own_rows = mine.shape[0]
    per_dev = new_ref.shape[0]
    blocks = 4 * parts
    own_block = (z * 4 + place.dp) * 2 + y
    quarter, across = x * 2 + c, (1 - x) * 2 + c
    partner, x_side, y_side = place.at(c=1 - c), place.at(x=1 - x), place.at(y=1 - y)
    up, down = place.at(z=jnp.minimum(z + 1, deep - 1)), place.at(z=jnp.maximum(z - 1, 0))
    outer = (z == 0) | (z == 3)
    inner = (z == 1) | (z == 2)
    mate_z = z + 1 - 2 * (z % 2)
    mate = place.at(z=mate_z)
    far = [3 - 3 * (z // 2), 2 - z // 2]
    dests = far + [mate_z, z]

    loads = [
        pltpu.make_async_copy(ids_hbm, ids, load_sems.at[0]),
        pltpu.make_async_copy(table_hbm, table, load_sems.at[1]),
    ]
    for q in range(4):
        part = qkv_hbm.at[:, pl.ds(q * width, width)] if q < 3 else out_w_hbm
        loads.append(pltpu.make_async_copy(part, w.at[q, own], load_sems.at[2 + q]))
    loads.append(pltpu.make_async_copy(gain_hbm, gain, load_sems.at[6]))
    loads.append(pltpu.make_async_copy(bias_hbm, bias, load_sems.at[7]))
    loads.append(pltpu.make_async_copy(assign_hbm, assign, load_sems.at[8]))
    loads.append(
        pltpu.make_async_copy(
            cent_hbm.at[:, pl.ds(pl.multiple_of(own * per_dev, 128), per_dev)], cent.at[own], load_sems.at[9]
        )
    )
    for load in loads:
        load.start()
    place.greet()
    loads[0].wait()
    columns = ids[...].T
    for k in range(parts):
        id_columns[k // 2, k % 2] = columns[:, k : k + 1]
    loads[1].wait()

    def look(y0):
        local = id_columns[:, y0].reshape(deep * own_rows, 1) - own * vocab_rows
        hot = local == lax.broadcasted_iota(jnp.int32, (deep * own_rows, vocab_rows), 1)
        found = jnp.dot(
            jnp.where(hot, 1.0, 0.0).astype(jnp.bfloat16), table[...], preferred_element_type=jnp.float32
        )
        rows[y0] = found.astype(jnp.bfloat16).reshape(deep, own_rows, width)

    base = (place.dp * parts + own) * per_dev
    centroid = lax.broadcasted_iota(jnp.int32, (per_dev, 2 * own_rows), 0) + base

    def prepare(z1):
        @pl.loop(0, 4)
        def each(i):
            ones = jnp.where(centroid == assign[i * deep + z1], 1.0, 0.0)
            hot[z1, :, pl.ds(pl.multiple_of(i * 2 * own_rows, 128), 2 * own_rows)] = ones.astype(jnp.bfloat16)
            counts[...] += jnp.sum(ones, axis=1, keepdims=True)

    counts[...] = jnp.zeros_like(counts)
    look(1 - y)
    for load in loads[2:]:
        load.wait()
    place.met()
    out = Sender(send_sems)

    def send_rows(to):
        out.send(rows.at[1 - y, to], from_y.at[to], y_sems.at[to], y_side)

    def w_send(q, s, peer, when=None):
        out.send(w.at[q, s], w.at[q, s], w_sems.at[q, s], peer, when)

    def w_wait(q, s):
        out.arrived(w.at[q, s], w_sems.at[q, s], partner)

    def give(z0, y0, when=None):
        to = z0 * 2 + y0
        part = pl.ds(pl.multiple_of(to * per_dev, 128), per_dev)
        out.send(
            cent_hbm.at[:, part], cent.at[own], cent_sems.at[own], {"dp": place.dp, "fsdp": to}, when
        )

    w_send(quarter, own, up, z + 1 < deep)
    w_send(quarter, own, down, z > 0)
    send_rows(dests[0])
    send_rows(dests[1])
    w_send(quarter, own, y_side)
    send_rows(dests[2])
    send_rows(dests[3])
    give(mate_z, y)
    give(3 - z, y, inner)
    look(y)
    prepare(0)

    def w_column(k):
        z0 = near_first(z, k, deep)
        s = z0 * 2 + y
        w_wait(quarter, s)
        w_send(quarter, s, up, (z0 < z) & (z + 1 < deep))
        w_send(quarter, s, down, (z0 > z) & (z > 0))
        w_send(quarter, s, y_side)
        w_send(quarter, s, x_side)
        w_send(quarter, s, partner)

    def join(to):
        out.arrived(from_y.at[to], y_sems.at[to], y_side)
        joined_y[to] = from_y[to] + rows[y, to]

    def hand(to, when):
        out.send(joined_y.at[to], from_mate.at[to], mate_sems.at[to], mate, when)

    def mate_arrived(to, when):
        out.arrived(from_mate.at[to], mate_sems.at[to], mate, when)

    w_column(1)
    join(dests[0])
    hand(dests[0], outer)
    w_column(2)
    prepare(1)
    join(dests[1])
    hand(dests[1], outer)

    def onward(to):
        mate_arrived(to, inner)

        @pl.when(inner)
        def add():
            joined_y[to] = joined_y[to] + from_mate[to]

        out.send(joined_y.at[to], from_far, far_sems.at[0], place.at(z=to), inner)

    onward(dests[0])
    w_column(3)
    prepare(2)
    join(dests[2])
    hand(dests[2], None)
    onward(dests[1])
    give((z + 2) % deep, y)
    give(3 - z, y, outer)
    join(dests[3])
    prepare(3)
    for k in range(deep):
        s = near_first(z, k, deep) * 2 + (1 - y)
        w_wait(quarter, s)
        w_send(quarter, s, x_side)
        w_send(quarter, s, partner)
    for k in range(deep):
        give((z + k) % deep, 1 - y)
    others = [near_first(z, k, deep) * 2 + y for k in range(1, deep)]
    others += [near_first(z, k, deep) * 2 + (1 - y) for k in range(deep)]
    for s in others:
        w_wait(across, s)
        w_send(across, s, partner)
    mate_arrived(z, None)
    out.arrived(from_far, far_sems.at[0], mate)
    total = joined_y[z] + from_mate[z] + from_far[...]
    for q in (x * 2 + (1 - c), (1 - x) * 2 + (1 - c)):
        for s in others:
            w_wait(q, s)
    mine[...] = passage(total, range(4), gain[...], bias[...], w)

    x_first = c == 1
    second_xy = (jnp.where(x_first, 1 - x, x), jnp.where(x_first, y, 1 - y))
    third_xy = (jnp.where(x_first, x, 1 - x), jnp.where(x_first, 1 - y, y))
    second = place.at(x=second_xy[0], y=second_xy[1])
    third = place.at(x=third_xy[0], y=third_xy[1])

    def number(x0, c0, z0, y0):
        return (z0 * 4 + x0 * 2 + c0) * 2 + y0

    cut_rows = own_rows // CUTS

    def push(b, h, peer, when=None, src=None):
        lines = pl.ds(h * cut_rows, cut_rows)
        there = tokens.at[b, lines]
        out.send(there if src is None else src.at[lines], there, token_sems.at[b, h], peer, when)

    def wait(b, h):
        out.arrived(tokens.at[b, pl.ds(h * cut_rows, cut_rows)], token_sems.at[b, h], partner)

    for h in range(CUTS):
        push(own_block, h, up, z + 1 < deep, mine)
        push(own_block, h, down, z > 0, mine)
        for peer in (second, third, partner):
            push(own_block, h, peer, None, mine)
    tokens[own_block] = mine[...]

    def add_up(k, part, of):
        z1 = near_first(z, k, deep)
        span = pl.ds(part * per_dev // of, per_dev // of)
        term = jnp.dot(
            hot[z1, span, :],
            tokens[pl.ds(z1 * 8, 8)].reshape(8 * own_rows, width),
            preferred_element_type=jnp.float32,
        )
        if k == 0:
            new_ref[span, :] = term
        else:
            new_ref[span, :] += term

    def score(z1, i):
        first = z1 * 8 + i * 2
        logits = lax.dot_general(
            old[...],
            tokens[pl.ds(first, 2)].reshape(2 * own_rows, width),
            (((1,), (1,)), ((), ())),
            preferred_element_type=jnp.float32,
        )
        peak = jnp.max(logits, axis=0, keepdims=True)
        mass = jnp.sum(jnp.exp(logits - peak), axis=0, keepdims=True)
        hits = centroid == assign[i * deep + z1]
        pick = jnp.sum(jnp.where(hits, logits, 0.0), axis=0, keepdims=True)
        for half in range(2):
            at = slice(half * own_rows, (half + 1) * own_rows)
            for k, row in enumerate((peak, mass, pick)):
                stat[first + half, pl.ds(k, 1), :] = row[:, at]
            pl.when(first + half != own_block)(stat_copy(first + half).start)

    def scores(k, part, of):
        z1 = near_first(z, k, deep)

        @pl.loop(part * 4 // of, (part + 1) * 4 // of)
        def each(i):
            score(z1, i)

    def stat_copy(b):
        return pltpu.make_async_remote_copy(
            src_ref=stat.at[b],
            dst_ref=got.at[own_block],
            send_sem=stat_send.at[b],
            recv_sem=stat_recv.at[own_block],
            device_id={"dp": b % 8 // 2, "fsdp": b // 8 * 2 + b % 2},
            device_id_type=pl.DeviceIdType.MESH,
        )

    def take_centroids():
        for k in range(1, parts):
            s = (own + k) % parts
            out.arrived(cent.at[s], cent_sems.at[s], partner)
        old[...] = cent[...].reshape(width, per_dev).T

    def onward_z(k):
        z0 = near_first(z, k, deep)
        b = number(x, c, z0, y)
        for h in range(CUTS):
            wait(b, h)
            push(b, h, up, (z0 < z) & (z + 1 < deep))
            push(b, h, down, (z0 > z) & (z > 0))
            push(b, h, second)
            push(b, h, third)
            push(b, h, partner)

    def onward_second(k):
        b = number(second_xy[0], c, near_first(z, k, deep), second_xy[1])
        for h in range(CUTS):
            wait(b, h)
            push(b, h, third)
            push(b, h, partner)

    def finish(k):
        z1 = near_first(z, k, deep)
        for xx, yy in (third_xy, (1 - x, 1 - y)):
            b = number(xx, c, z1, yy)
            for h in range(CUTS):
                wait(b, h)
                push(b, h, partner)

    def theirs(k):
        z1 = near_first(z, k, deep)
        for x0 in range(2):
            for y0 in range(2):
                for h in range(CUTS):
                    wait(number(x0, 1 - c, z1, y0), h)

    take_centroids()
    onward_second(0)
    onward_z(1)
    finish(0)
    onward_second(1)
    theirs(0)
    add_up(0, 0, 1)
    scores(0, 0, 2)
    onward_z(2)
    finish(1)
    scores(0, 1, 2)
    onward_second(2)
    theirs(1)
    add_up(1, 0, 1)
    scores(1, 0, 2)
    onward_z(3)
    finish(2)
    scores(1, 1, 2)
    onward_second(3)
    theirs(2)
    add_up(2, 0, 1)
    scores(2, 0, 2)
    finish(3)
    scores(2, 1, 2)
    theirs(3)
    add_up(3, 0, 1)
    scores(3, 0, 1)

    many = counts[...]
    new_ref[...] = jnp.where(
        many > 0, new_ref[...] / jnp.maximum(many, 1.0), old[...].astype(jnp.float32)
    )
    got[own_block] = stat[own_block]

    @pl.loop(0, blocks)
    def each_device(b):
        @pl.when(b != own_block)
        def done():
            stat_copy(b).wait_send()
            pltpu.make_async_remote_copy(
                src_ref=got.at[b],
                dst_ref=got.at[b],
                send_sem=stat_send.at[b],
                recv_sem=stat_recv.at[b],
                device_id=partner,
                device_id_type=pl.DeviceIdType.MESH,
            ).wait_recv()

    peaks, masses, picks = (got[:, k, :] for k in range(3))
    top = jnp.max(peaks, axis=0, keepdims=True)
    mass = jnp.sum(masses * jnp.exp(peaks - top), axis=0, keepdims=True)
    loss_ref[...] = jnp.log(mass) + top - jnp.sum(picks, axis=0, keepdims=True)
    out.drain()


def token_shards(token_ids, embed_table, w_qkv, w_out, ln_gain, ln_bias, centroids_t, assignments):
    parts = lax.axis_size("fsdp")
    deep = parts // 2
    blocks = 4 * parts
    width = embed_table.shape[1]
    feats = w_qkv.shape[0]
    own_rows = token_ids.shape[0] // parts
    per_dev = centroids_t.shape[1] // parts
    half = jnp.bfloat16
    block = (own_rows, width)
    sems = pltpu.SemaphoreType.DMA
    in_hbm = pl.BlockSpec(memory_space=pltpu.HBM)
    loss, new = pl.pallas_call(
        functools.partial(step_kernel, deep),
        out_shape=(
            jax.ShapeDtypeStruct((1, own_rows), jnp.float32),
            jax.ShapeDtypeStruct((per_dev, width), jnp.float32),
        ),
        in_specs=[in_hbm] * 8,
        out_specs=(WHOLE_VMEM, WHOLE_VMEM),
        scratch_shapes=[
            pltpu.VMEM((parts, own_rows), jnp.int32),
            pltpu.VMEM(embed_table.shape, half),
            pltpu.VMEM((1, width), jnp.float32),
            pltpu.VMEM((1, width), jnp.float32),
            pltpu.VMEM((blocks // 2, 1, 2 * own_rows), jnp.int32),
            pltpu.VMEM((deep, 2, own_rows, 1), jnp.int32),
            pltpu.VMEM((2, deep, *block), half),
            pltpu.VMEM((4, parts, feats, width), half),
            pltpu.VMEM((deep, *block), half),
            pltpu.VMEM((deep, *block), half),
            pltpu.VMEM((deep, *block), half),
            pltpu.VMEM(block, half),
            pltpu.VMEM((parts, feats, per_dev), half),
            pltpu.VMEM((per_dev, width), half),
            pltpu.VMEM(block, half),
            pltpu.VMEM((blocks, *block), half),
            pltpu.VMEM((deep, per_dev, 8 * own_rows), half),
            pltpu.VMEM((per_dev, 1), jnp.float32),
            pltpu.VMEM((blocks, 8, own_rows), jnp.float32),
            pltpu.VMEM((blocks, 8, own_rows), jnp.float32),
            sems((10,)),
            sems((64 * deep,)),
            sems((deep,)),
            sems((deep,)),
            sems((1,)),
            sems((4, parts)),
            sems((parts,)),
            sems((blocks, CUTS)),
            sems((blocks,)),
            sems((blocks,)),
        ],
        compiler_params=pltpu.CompilerParams(
            collective_id=0, has_side_effects=True, vmem_limit_bytes=VMEM_LIMIT
        ),
        name="whole_step",
    )(
        *(
            pltpu.with_memory_space_constraint(array, pltpu.HBM)
            for array in (
                token_ids.reshape(parts, own_rows),
                embed_table,
                w_qkv,
                w_out,
                ln_gain.reshape(1, width),
                ln_bias.reshape(1, width),
                centroids_t,
                assignments.reshape(blocks // 2, 1, 2 * own_rows),
            )
        )
    )
    return loss.reshape(own_rows), new


def plan(mesh):
    dp_size, fsdp_size = mesh.shape["dp"], mesh.shape["fsdp"]

    def either(*args):
        few_tokens = args[7].shape[0] <= args[6].shape[1]
        paired = dp_size == 4 and fsdp_size == 8
        return token_shards(*args) if few_tokens and paired else shards(*args)

    return either


def solution(mesh):
    return jax.shard_map(
        plan(mesh),
        mesh=mesh,
        in_specs=(
            P("dp"),
            P("fsdp", None),
            P("fsdp", None),
            P("fsdp", None),
            P(),
            P(),
            P("fsdp", "dp"),
            P(),
        ),
        out_specs=(P(("dp", "fsdp")), P(("dp", "fsdp"), None)),
        check_vma=False,
    )
```

```python
import functools
import math

import jax
import jax.numpy as jnp
from jax import lax
from jax.experimental import pallas as pl
from jax.experimental.pallas import tpu as pltpu
from jax.sharding import PartitionSpec as P

HEADS = 12
HEAD = 64
SEQ = 128


def joined(shard, axis, combine):
    everything = jax.tree.map(lambda part: lax.all_gather(part, axis), shard)
    initial = jax.tree.map(lambda part: part[0], everything)

    def lap(k, so_far):
        return combine(so_far, jax.tree.map(lambda part: part[k], everything))

    return lax.fori_loop(1, lax.axis_size(axis), lap, initial)


def layer_norm(values, ln_gain, ln_bias):
    center = values - jnp.mean(values, axis=-1, keepdims=True)
    spread = jnp.mean(center * center, axis=-1, keepdims=True)
    return center * lax.rsqrt(spread + 1e-05) * ln_gain + ln_bias


def encode(inputs, qkv_full, out_full, ln_gain, ln_bias):
    passages = inputs.shape[0] // SEQ
    packed = jnp.dot(inputs, qkv_full, preferred_element_type=jnp.float32).astype(jnp.bfloat16)
    packed = packed.reshape(passages, SEQ, 3, HEADS, HEAD)
    scores = jnp.einsum(
        "bqhd,bkhd->bhqk", packed[:, :, 0], packed[:, :, 1], preferred_element_type=jnp.float32
    ) * (1.0 / math.sqrt(HEAD))
    probs = jax.nn.softmax(scores, axis=-1).astype(jnp.bfloat16)
    context = jnp.einsum(
        "bhqk,bkhd->bqhd", probs, packed[:, :, 2], preferred_element_type=jnp.float32
    )
    context = context.astype(jnp.bfloat16).reshape(inputs.shape[0], HEADS * HEAD)
    mixed = jnp.dot(context, out_full, preferred_element_type=jnp.float32) + inputs.astype(
        jnp.float32
    )
    return layer_norm(mixed, ln_gain, ln_bias).astype(jnp.bfloat16)


def one_hot_sums(rows, targets, width):
    count = rows.shape[0]
    step_rows = math.gcd(count, 512)
    columns = jnp.arange(width, dtype=jnp.int32)

    def one_visit(totals, pieces):
        block_rows, block_targets = pieces
        hits = (block_targets[:, None] == columns[None, :]).astype(jnp.bfloat16)
        return (
            totals
            + lax.dot_general(
                hits, block_rows, (((0,), (0,)), ((), ())), preferred_element_type=jnp.float32
            ),
            None,
        )

    start = jnp.zeros((width, rows.shape[1]), jnp.float32)
    totals, unused = lax.scan(
        one_visit,
        start,
        (
            rows.reshape(count // step_rows, step_rows, rows.shape[1]),
            targets.reshape(count // step_rows, step_rows),
        ),
    )
    return totals


def combine_parts(first, second):
    peak = jnp.maximum(first[0], second[0])
    mass = first[1] * jnp.exp(first[0] - peak) + second[1] * jnp.exp(second[0] - peak)
    return (peak, mass, first[2] + second[2])


def shards(token_ids, embed_table, w_qkv, w_out, ln_gain, ln_bias, centroids_t, assignments):
    dp_size = lax.axis_size("dp")
    fsdp_size = lax.axis_size("fsdp")
    dp_rank = lax.axis_index("dp")
    fsdp_rank = lax.axis_index("fsdp")
    vocab_rows = embed_table.shape[0]
    local_ids = token_ids - fsdp_rank * vocab_rows
    inside = (local_ids >= 0) & (local_ids < vocab_rows)
    looked = jnp.take(embed_table, jnp.clip(local_ids, 0, vocab_rows - 1), axis=0)
    looked = jnp.where(inside[:, None], looked, jnp.zeros_like(looked))
    inputs = (
        lax.psum_scatter(looked, "fsdp", scatter_dimension=0, tiled=True)
        .astype(jnp.float32)
        .astype(jnp.bfloat16)
    )
    qkv_full, out_full, cent_full = (
        lax.all_gather(w_qkv, "fsdp", axis=0, tiled=True),
        lax.all_gather(w_out, "fsdp", axis=0, tiled=True),
        lax.all_gather(centroids_t, "fsdp", axis=0, tiled=True),
    )
    encoded = encode(inputs, qkv_full, out_full, ln_gain, ln_bias)
    own_rows = encoded.shape[0]
    width = encoded.shape[1]
    block_width = cent_full.shape[1]
    per_dev = block_width // fsdp_size
    slab = lax.all_gather(encoded, "dp", axis=0, tiled=True)
    slab_assign = lax.dynamic_index_in_dim(
        assignments.reshape(dp_size, fsdp_size, own_rows), fsdp_rank, 1, keepdims=False
    ).reshape(-1)
    owned = slab_assign - dp_rank * block_width
    slab_rows = slab.shape[0]
    step_rows = math.gcd(slab_rows, 512)
    columns = jnp.arange(block_width, dtype=jnp.int32)

    def body_visit(totals, pieces):
        block_rows, local = pieces
        logits = jnp.dot(block_rows, cent_full, preferred_element_type=jnp.float32)
        peak = jnp.max(logits, axis=1)
        mass = jnp.sum(jnp.exp(logits - peak[:, None]), axis=1)
        hits = local[:, None] == columns[None, :]
        picked = jnp.sum(jnp.where(hits, logits, 0.0), axis=1)
        return (totals, (peak, mass, picked))

    start = jnp.zeros((1,), jnp.float32)
    partial_value, stats = lax.scan(
        body_visit,
        start,
        (
            slab.reshape(slab_rows // step_rows, step_rows, width),
            owned.reshape(slab_rows // step_rows, step_rows),
        ),
    )
    peaks, masses, picks = (stats[0].reshape(-1), stats[1].reshape(-1), stats[2].reshape(-1))
    peaks, masses, picks = joined((peaks, masses, picks), "dp", combine_parts)
    peak_own = lax.dynamic_slice_in_dim(peaks, dp_rank * own_rows, own_rows)
    mass_own = lax.dynamic_slice_in_dim(masses, dp_rank * own_rows, own_rows)
    pick_own = lax.dynamic_slice_in_dim(picks, dp_rank * own_rows, own_rows)
    token_loss = jnp.log(mass_own) + peak_own - pick_own
    share = lax.all_to_all(encoded, "fsdp", split_axis=1, concat_axis=0, tiled=True)
    every_rows = lax.all_gather(share, "dp", axis=0, tiled=True)
    block_local = assignments - dp_rank * block_width
    partial_share = one_hot_sums(every_rows, block_local, block_width)
    totals = lax.all_to_all(partial_share, "fsdp", split_axis=0, concat_axis=1, tiled=True)
    base = dp_rank * block_width + fsdp_rank * per_dev
    targets = base + jnp.arange(per_dev, dtype=jnp.int32)
    counts = jnp.sum((assignments[:, None] == targets[None, :]).astype(jnp.int32), axis=0)
    previous = lax.dynamic_slice_in_dim(cent_full, fsdp_rank * per_dev, per_dev, 1).T.astype(
        jnp.float32
    )
    new_centroids = jnp.where(
        counts[:, None] > 0, totals / jnp.maximum(counts, 1)[:, None].astype(jnp.float32), previous
    )
    return (token_loss, new_centroids)


VMEM_LIMIT = 46 * 1024 * 1024
CUTS = 2
WHOLE_VMEM = pl.BlockSpec(memory_space=pltpu.VMEM)


class Place:
    def __init__(self, deep):
        self.deep = deep
        self.dp, self.fsdp = lax.axis_index("dp"), lax.axis_index("fsdp")
        self.x, self.c = self.dp // 2, self.dp % 2
        self.z, self.y = self.fsdp // 2, self.fsdp % 2

    def at(self, x=None, c=None, z=None, y=None):
        x, c = self.x if x is None else x, self.c if c is None else c
        z, y = self.z if z is None else z, self.y if y is None else y
        return {"dp": x * 2 + c, "fsdp": z * 2 + y}

    def greet(self):
        barrier = pltpu.get_barrier_semaphore()
        everyone = 8 * self.deep
        me = self.dp * 2 * self.deep + self.fsdp

        @pl.loop(1, everyone)
        def each(k):
            peer = (me + k) % everyone
            there = {"dp": peer // (2 * self.deep), "fsdp": peer % (2 * self.deep)}
            pl.semaphore_signal(barrier, inc=1, device_id=there, device_id_type=pl.DeviceIdType.MESH)

    def met(self):
        pl.semaphore_wait(pltpu.get_barrier_semaphore(), 8 * self.deep - 1)


class Sender:
    def __init__(self, sems):
        self.sems, self.used, self.sent = sems, 0, []

    def send(self, src, dst, recv_sem, peer, when=None):
        copy = pltpu.make_async_remote_copy(
            src_ref=src,
            dst_ref=dst,
            send_sem=self.sems.at[self.used],
            recv_sem=recv_sem,
            device_id=peer,
            device_id_type=pl.DeviceIdType.MESH,
        )
        self.used += 1
        self.sent.append((copy, when))
        guarded(when, copy.start)

    def arrived(self, dst, recv_sem, peer, when=None):
        copy = pltpu.make_async_remote_copy(
            src_ref=dst,
            dst_ref=dst,
            send_sem=self.sems.at[0],
            recv_sem=recv_sem,
            device_id=peer,
            device_id_type=pl.DeviceIdType.MESH,
        )
        guarded(when, copy.wait_recv)

    def drain(self):
        for copy, when in self.sent:
            guarded(when, copy.wait_send)


def guarded(when, action):
    if when is None:
        action()
    else:
        pl.when(when)(action)


def near_first(z, k, deep):
    below, above = z, deep - 1 - z
    both = jnp.minimum(below, above)
    swing = z - (k + 1) // 2 if k % 2 else z + k // 2
    far = jnp.where(above > below, z + k - both, z - k + both)
    return jnp.where(k <= 2 * both, swing, far)


def passage(x, quarters, gain, bias, w_ref):
    width = x.shape[1]

    def dense(rows, q):
        weights = w_ref[q].reshape(width, width)
        return jnp.dot(rows, weights, preferred_element_type=jnp.float32)

    query, key, value = (dense(x, q).astype(jnp.bfloat16) for q in quarters[:3])
    context = []
    for head in range(HEADS):
        at = slice(head * HEAD, (head + 1) * HEAD)
        scores = lax.dot_general(
            query[:, at], key[:, at], (((1,), (1,)), ((), ())), preferred_element_type=jnp.float32
        ) * (1.0 / math.sqrt(HEAD))
        weight = jnp.exp(scores - jnp.max(scores, axis=1, keepdims=True))
        probs = (weight / jnp.sum(weight, axis=1, keepdims=True)).astype(jnp.bfloat16)
        context.append(jnp.dot(probs, value[:, at], preferred_element_type=jnp.float32))
    context = jnp.concatenate(context, axis=1).astype(jnp.bfloat16)
    mixed = dense(context, quarters[3]) + x.astype(jnp.float32)
    return layer_norm(mixed, gain, bias).astype(jnp.bfloat16)


def step_kernel(
    deep,
    ids_hbm,
    table_hbm,
    qkv_hbm,
    out_w_hbm,
    gain_hbm,
    bias_hbm,
    cent_hbm,
    assign_hbm,
    loss_ref,
    new_ref,
    ids,
    table,
    gain,
    bias,
    assign,
    assign_plane,
    id_columns,
    rows,
    w,
    from_y,
    joined_y,
    from_mate,
    from_far,
    cent,
    old,
    mine,
    tokens,
    hot,
    counts,
    stat,
    got,
    load_sems,
    send_sems,
    y_sems,
    mate_sems,
    far_sems,
    w_sems,
    cent_sems,
    token_sems,
    stat_send,
    stat_recv,
):
    place = Place(deep)
    x, c, z, y = place.x, place.c, place.z, place.y
    own = place.fsdp
    parts = 2 * deep
    vocab_rows, width = table.shape
    own_rows = mine.shape[0]
    per_dev = new_ref.shape[0]
    blocks = 4 * parts
    own_block = (z * 4 + place.dp) * 2 + y
    quarter, across = x * 2 + c, (1 - x) * 2 + c
    partner, x_side, y_side = place.at(c=1 - c), place.at(x=1 - x), place.at(y=1 - y)
    up, down = place.at(z=jnp.minimum(z + 1, deep - 1)), place.at(z=jnp.maximum(z - 1, 0))
    outer = (z == 0) | (z == 3)
    inner = (z == 1) | (z == 2)
    mate_z = z + 1 - 2 * (z % 2)
    mate = place.at(z=mate_z)
    far = [3 - 3 * (z // 2), 2 - z // 2]
    dests = far + [mate_z, z]

    loads = [
        pltpu.make_async_copy(ids_hbm, ids, load_sems.at[0]),
        pltpu.make_async_copy(table_hbm, table, load_sems.at[1]),
    ]
    for q in range(4):
        part = qkv_hbm.at[:, pl.ds(q * width, width)] if q < 3 else out_w_hbm
        loads.append(pltpu.make_async_copy(part, w.at[q, own], load_sems.at[2 + q]))
    loads.append(pltpu.make_async_copy(gain_hbm, gain, load_sems.at[6]))
    loads.append(pltpu.make_async_copy(bias_hbm, bias, load_sems.at[7]))
    loads.append(pltpu.make_async_copy(assign_hbm, assign, load_sems.at[8]))
    loads.append(
        pltpu.make_async_copy(
            cent_hbm.at[:, pl.ds(pl.multiple_of(own * per_dev, 128), per_dev)], cent.at[own], load_sems.at[9]
        )
    )
    for load in loads:
        load.start()
    place.greet()
    loads[0].wait()
    columns = ids[...].T
    for k in range(parts):
        id_columns[k // 2, k % 2] = columns[:, k : k + 1]
    loads[1].wait()

    def look(y0):
        local = id_columns[:, y0].reshape(deep * own_rows, 1) - own * vocab_rows
        hot = local == lax.broadcasted_iota(jnp.int32, (deep * own_rows, vocab_rows), 1)
        found = jnp.dot(
            jnp.where(hot, 1.0, 0.0).astype(jnp.bfloat16), table[...], preferred_element_type=jnp.float32
        )
        rows[y0] = found.astype(jnp.bfloat16).reshape(deep, own_rows, width)

    base = (place.dp * parts + own) * per_dev
    centroid = lax.broadcasted_iota(jnp.int32, (per_dev, 2 * own_rows), 0) + base

    def prepare(z1):
        for i in range(4):
            assign_plane[z1, :, i * 2 * own_rows : (i + 1) * 2 * own_rows] = assign[i * deep + z1]

        @pl.loop(0, 4)
        def each(i):
            ones = jnp.where(centroid == assign[i * deep + z1], 1.0, 0.0)
            hot[z1, :, pl.ds(pl.multiple_of(i * 2 * own_rows, 128), 2 * own_rows)] = ones.astype(jnp.bfloat16)
            counts[...] += jnp.sum(ones, axis=1, keepdims=True)

    counts[...] = jnp.zeros_like(counts)
    look(1 - y)
    for load in loads[2:]:
        load.wait()
    place.met()
    out = Sender(send_sems)

    def send_rows(to):
        out.send(rows.at[1 - y, to], from_y.at[to], y_sems.at[to], y_side)

    def w_send(q, s, peer, when=None):
        out.send(w.at[q, s], w.at[q, s], w_sems.at[q, s], peer, when)

    def w_wait(q, s):
        out.arrived(w.at[q, s], w_sems.at[q, s], partner)

    def give(z0, y0, when=None):
        to = z0 * 2 + y0
        part = pl.ds(pl.multiple_of(to * per_dev, 128), per_dev)
        out.send(
            cent_hbm.at[:, part], cent.at[own], cent_sems.at[own], {"dp": place.dp, "fsdp": to}, when
        )

    w_send(quarter, own, up, z + 1 < deep)
    w_send(quarter, own, down, z > 0)
    send_rows(dests[0])
    send_rows(dests[1])
    w_send(quarter, own, y_side)
    send_rows(dests[2])
    send_rows(dests[3])
    give(mate_z, y)
    give(3 - z, y, inner)
    look(y)
    prepare(0)

    def w_column(k):
        z0 = near_first(z, k, deep)
        s = z0 * 2 + y
        w_wait(quarter, s)
        w_send(quarter, s, up, (z0 < z) & (z + 1 < deep))
        w_send(quarter, s, down, (z0 > z) & (z > 0))
        w_send(quarter, s, y_side)
        w_send(quarter, s, x_side)
        w_send(quarter, s, partner)

    def join(to):
        out.arrived(from_y.at[to], y_sems.at[to], y_side)
        joined_y[to] = from_y[to] + rows[y, to]

    def hand(to, when):
        out.send(joined_y.at[to], from_mate.at[to], mate_sems.at[to], mate, when)

    def mate_arrived(to, when):
        out.arrived(from_mate.at[to], mate_sems.at[to], mate, when)

    w_column(1)
    join(dests[0])
    hand(dests[0], outer)
    w_column(2)
    prepare(1)
    give(3 - z, 1 - y)
    join(dests[1])
    hand(dests[1], outer)

    def onward(to):
        mate_arrived(to, inner)

        @pl.when(inner)
        def add():
            joined_y[to] = joined_y[to] + from_mate[to]

        out.send(joined_y.at[to], from_far, far_sems.at[0], place.at(z=to), inner)

    onward(dests[0])
    w_column(3)
    prepare(2)
    join(dests[2])
    hand(dests[2], None)
    onward(dests[1])
    give((z + 2) % deep, y)
    give(3 - z, y, outer)
    join(dests[3])
    prepare(3)
    for k in range(deep):
        s = near_first(z, k, deep) * 2 + (1 - y)
        w_wait(quarter, s)
        w_send(quarter, s, x_side)
        w_send(quarter, s, partner)
    give((z + 2) % deep, 1 - y)
    give(mate_z, 1 - y)
    give(z, 1 - y)
    others = [near_first(z, k, deep) * 2 + y for k in range(1, deep)]
    others += [near_first(z, k, deep) * 2 + (1 - y) for k in range(deep)]
    for s in others:
        w_wait(across, s)
        w_send(across, s, partner)
    mate_arrived(z, None)
    out.arrived(from_far, far_sems.at[0], mate)
    total = joined_y[z] + from_mate[z] + from_far[...]
    for q in (x * 2 + (1 - c), (1 - x) * 2 + (1 - c)):
        for s in others:
            w_wait(q, s)
    mine[...] = passage(total, range(4), gain[...], bias[...], w)

    x_first = c == 1
    second_xy = (jnp.where(x_first, 1 - x, x), jnp.where(x_first, y, 1 - y))
    third_xy = (jnp.where(x_first, x, 1 - x), jnp.where(x_first, 1 - y, y))
    second = place.at(x=second_xy[0], y=second_xy[1])
    third = place.at(x=third_xy[0], y=third_xy[1])

    def number(x0, c0, z0, y0):
        return (z0 * 4 + x0 * 2 + c0) * 2 + y0

    cut_rows = own_rows // CUTS

    def push(b, h, peer, when=None, src=None):
        lines = pl.ds(h * cut_rows, cut_rows)
        there = tokens.at[b, lines]
        out.send(there if src is None else src.at[lines], there, token_sems.at[b, h], peer, when)

    def wait(b, h):
        out.arrived(tokens.at[b, pl.ds(h * cut_rows, cut_rows)], token_sems.at[b, h], partner)

    for h in range(CUTS):
        push(own_block, h, up, z + 1 < deep, mine)
        push(own_block, h, down, z > 0, mine)
        for peer in (second, third, partner):
            push(own_block, h, peer, None, mine)
    tokens[own_block] = mine[...]

    def add_up(k, part, of):
        z1 = near_first(z, k, deep)
        span = pl.ds(part * per_dev // of, per_dev // of)
        term = jnp.dot(
            hot[z1, span, :],
            tokens[pl.ds(z1 * 8, 8)].reshape(8 * own_rows, width),
            preferred_element_type=jnp.float32,
        )
        if k == 0:
            new_ref[span, :] = term
        else:
            new_ref[span, :] += term

    def scores(k):
        z1 = near_first(z, k, deep)
        plane = tokens[pl.ds(z1 * 8, 8)].reshape(8 * own_rows, width)
        chunk = math.gcd(per_dev, 256)
        target = assign_plane[z1] - base

        def logits_of(first):
            return lax.dot_general(
                old[first : first + chunk, :], plane, (((1,), (1,)), ((), ())), preferred_element_type=jnp.float32
            )

        line = lax.broadcasted_iota(jnp.int32, (chunk, 8 * own_rows), 0)
        later = logits_of(0)
        for first in range(0, per_dev, chunk):
            logits = later
            if first + chunk < per_dev:
                later = logits_of(first + chunk)
            top = jnp.max(logits, axis=0, keepdims=True)
            found = jnp.sum(jnp.where(line == target - first, logits, 0.0), axis=0, keepdims=True)
            if first == 0:
                peak, pick = top, found
                mass = jnp.sum(jnp.exp(logits - peak), axis=0, keepdims=True)
            else:
                higher = jnp.maximum(peak, top)
                mass = mass * jnp.exp(peak - higher) + jnp.sum(
                    jnp.exp(logits - higher), axis=0, keepdims=True
                )
                peak, pick = higher, pick + found
        for i in range(8):
            at = slice(i * own_rows, (i + 1) * own_rows)
            for n, row in enumerate((peak, mass, pick)):
                stat[z1 * 8 + i, pl.ds(n, 1), :] = row[:, at]

        @pl.loop(0, 8)
        def tell(i):
            b = z1 * 8 + i
            pl.when(b != own_block)(stat_copy(b).start)

    def stat_copy(b):
        return pltpu.make_async_remote_copy(
            src_ref=stat.at[b],
            dst_ref=got.at[own_block],
            send_sem=stat_send.at[b],
            recv_sem=stat_recv.at[own_block],
            device_id={"dp": b % 8 // 2, "fsdp": b // 8 * 2 + b % 2},
            device_id_type=pl.DeviceIdType.MESH,
        )

    def take_centroids():
        for k in range(1, parts):
            s = (own + k) % parts
            out.arrived(cent.at[s], cent_sems.at[s], partner)
        old[...] = cent[...].reshape(width, per_dev).T

    def onward_z(k):
        z0 = near_first(z, k, deep)
        b = number(x, c, z0, y)
        for h in range(CUTS):
            wait(b, h)
            push(b, h, up, (z0 < z) & (z + 1 < deep))
            push(b, h, down, (z0 > z) & (z > 0))
            push(b, h, second)
            push(b, h, third)
            push(b, h, partner)

    def onward_second(k):
        b = number(second_xy[0], c, near_first(z, k, deep), second_xy[1])
        for h in range(CUTS):
            wait(b, h)
            push(b, h, third)
            push(b, h, partner)

    def finish(k):
        z1 = near_first(z, k, deep)
        for xx, yy in (third_xy, (1 - x, 1 - y)):
            b = number(xx, c, z1, yy)
            for h in range(CUTS):
                wait(b, h)
                push(b, h, partner)

    def theirs(k):
        z1 = near_first(z, k, deep)
        for x0 in range(2):
            for y0 in range(2):
                for h in range(CUTS):
                    wait(number(x0, 1 - c, z1, y0), h)

    onward_z(1)
    onward_second(0)
    onward_z(2)
    onward_second(1)
    onward_z(3)
    finish(0)
    onward_second(2)
    finish(1)
    onward_second(3)
    theirs(0)
    take_centroids()
    add_up(0, 0, 1)
    scores(0)
    finish(2)
    theirs(1)
    add_up(1, 0, 1)
    scores(1)
    finish(3)
    theirs(2)
    add_up(2, 0, 1)
    scores(2)
    theirs(3)
    add_up(3, 0, 1)
    scores(3)

    many = counts[...]
    new_ref[...] = jnp.where(
        many > 0, new_ref[...] / jnp.maximum(many, 1.0), old[...].astype(jnp.float32)
    )
    got[own_block] = stat[own_block]

    @pl.loop(0, blocks)
    def each_device(b):
        @pl.when(b != own_block)
        def done():
            stat_copy(b).wait_send()
            pltpu.make_async_remote_copy(
                src_ref=got.at[b],
                dst_ref=got.at[b],
                send_sem=stat_send.at[b],
                recv_sem=stat_recv.at[b],
                device_id=partner,
                device_id_type=pl.DeviceIdType.MESH,
            ).wait_recv()

    peaks, masses, picks = (got[:, k, :] for k in range(3))
    top = jnp.max(peaks, axis=0, keepdims=True)
    mass = jnp.sum(masses * jnp.exp(peaks - top), axis=0, keepdims=True)
    loss_ref[...] = jnp.log(mass) + top - jnp.sum(picks, axis=0, keepdims=True)
    out.drain()


def token_shards(token_ids, embed_table, w_qkv, w_out, ln_gain, ln_bias, centroids_t, assignments):
    parts = lax.axis_size("fsdp")
    deep = parts // 2
    blocks = 4 * parts
    width = embed_table.shape[1]
    feats = w_qkv.shape[0]
    own_rows = token_ids.shape[0] // parts
    per_dev = centroids_t.shape[1] // parts
    half = jnp.bfloat16
    block = (own_rows, width)
    sems = pltpu.SemaphoreType.DMA
    in_hbm = pl.BlockSpec(memory_space=pltpu.HBM)
    loss, new = pl.pallas_call(
        functools.partial(step_kernel, deep),
        out_shape=(
            jax.ShapeDtypeStruct((1, own_rows), jnp.float32),
            jax.ShapeDtypeStruct((per_dev, width), jnp.float32),
        ),
        in_specs=[in_hbm] * 8,
        out_specs=(WHOLE_VMEM, WHOLE_VMEM),
        scratch_shapes=[
            pltpu.VMEM((parts, own_rows), jnp.int32),
            pltpu.VMEM(embed_table.shape, half),
            pltpu.VMEM((1, width), jnp.float32),
            pltpu.VMEM((1, width), jnp.float32),
            pltpu.VMEM((blocks // 2, 1, 2 * own_rows), jnp.int32),
            pltpu.VMEM((deep, 1, 8 * own_rows), jnp.int32),
            pltpu.VMEM((deep, 2, own_rows, 1), jnp.int32),
            pltpu.VMEM((2, deep, *block), half),
            pltpu.VMEM((4, parts, feats, width), half),
            pltpu.VMEM((deep, *block), half),
            pltpu.VMEM((deep, *block), half),
            pltpu.VMEM((deep, *block), half),
            pltpu.VMEM(block, half),
            pltpu.VMEM((parts, feats, per_dev), half),
            pltpu.VMEM((per_dev, width), half),
            pltpu.VMEM(block, half),
            pltpu.VMEM((blocks, *block), half),
            pltpu.VMEM((deep, per_dev, 8 * own_rows), half),
            pltpu.VMEM((per_dev, 1), jnp.float32),
            pltpu.VMEM((blocks, 8, own_rows), jnp.float32),
            pltpu.VMEM((blocks, 8, own_rows), jnp.float32),
            sems((10,)),
            sems((64 * deep,)),
            sems((deep,)),
            sems((deep,)),
            sems((1,)),
            sems((4, parts)),
            sems((parts,)),
            sems((blocks, CUTS)),
            sems((blocks,)),
            sems((blocks,)),
        ],
        compiler_params=pltpu.CompilerParams(
            collective_id=0, has_side_effects=True, vmem_limit_bytes=VMEM_LIMIT
        ),
        name="whole_step",
    )(
        *(
            pltpu.with_memory_space_constraint(array, pltpu.HBM)
            for array in (
                token_ids.reshape(parts, own_rows),
                embed_table,
                w_qkv,
                w_out,
                ln_gain.reshape(1, width),
                ln_bias.reshape(1, width),
                centroids_t,
                assignments.reshape(blocks // 2, 1, 2 * own_rows),
            )
        )
    )
    return loss.reshape(own_rows), new


def plan(mesh):
    dp_size, fsdp_size = mesh.shape["dp"], mesh.shape["fsdp"]

    def either(*args):
        few_tokens = args[7].shape[0] <= args[6].shape[1]
        paired = dp_size == 4 and fsdp_size == 8
        return token_shards(*args) if few_tokens and paired else shards(*args)

    return either


def solution(mesh):
    return jax.shard_map(
        plan(mesh),
        mesh=mesh,
        in_specs=(
            P("dp"),
            P("fsdp", None),
            P("fsdp", None),
            P("fsdp", None),
            P(),
            P(),
            P("fsdp", "dp"),
            P(),
        ),
        out_specs=(P(("dp", "fsdp")), P(("dp", "fsdp"), None)),
        check_vma=False,
    )
```

```python
import functools
import math

import jax
import jax.numpy as jnp
from jax import lax
from jax.experimental import pallas as pl
from jax.experimental.pallas import tpu as pltpu
from jax.sharding import PartitionSpec as P

HEADS = 12
HEAD = 64
SEQ = 128


def joined(shard, axis, combine):
    everything = jax.tree.map(lambda part: lax.all_gather(part, axis), shard)
    initial = jax.tree.map(lambda part: part[0], everything)

    def lap(k, so_far):
        return combine(so_far, jax.tree.map(lambda part: part[k], everything))

    return lax.fori_loop(1, lax.axis_size(axis), lap, initial)


def layer_norm(values, ln_gain, ln_bias):
    center = values - jnp.mean(values, axis=-1, keepdims=True)
    spread = jnp.mean(center * center, axis=-1, keepdims=True)
    return center * lax.rsqrt(spread + 1e-05) * ln_gain + ln_bias


def encode(inputs, qkv_full, out_full, ln_gain, ln_bias):
    passages = inputs.shape[0] // SEQ
    packed = jnp.dot(inputs, qkv_full, preferred_element_type=jnp.float32).astype(jnp.bfloat16)
    packed = packed.reshape(passages, SEQ, 3, HEADS, HEAD)
    scores = jnp.einsum(
        "bqhd,bkhd->bhqk", packed[:, :, 0], packed[:, :, 1], preferred_element_type=jnp.float32
    ) * (1.0 / math.sqrt(HEAD))
    probs = jax.nn.softmax(scores, axis=-1).astype(jnp.bfloat16)
    context = jnp.einsum(
        "bhqk,bkhd->bqhd", probs, packed[:, :, 2], preferred_element_type=jnp.float32
    )
    context = context.astype(jnp.bfloat16).reshape(inputs.shape[0], HEADS * HEAD)
    mixed = jnp.dot(context, out_full, preferred_element_type=jnp.float32) + inputs.astype(
        jnp.float32
    )
    return layer_norm(mixed, ln_gain, ln_bias).astype(jnp.bfloat16)


def one_hot_sums(rows, targets, width):
    count = rows.shape[0]
    step_rows = math.gcd(count, 512)
    columns = jnp.arange(width, dtype=jnp.int32)

    def one_visit(totals, pieces):
        block_rows, block_targets = pieces
        hits = (block_targets[:, None] == columns[None, :]).astype(jnp.bfloat16)
        return (
            totals
            + lax.dot_general(
                hits, block_rows, (((0,), (0,)), ((), ())), preferred_element_type=jnp.float32
            ),
            None,
        )

    start = jnp.zeros((width, rows.shape[1]), jnp.float32)
    totals, unused = lax.scan(
        one_visit,
        start,
        (
            rows.reshape(count // step_rows, step_rows, rows.shape[1]),
            targets.reshape(count // step_rows, step_rows),
        ),
    )
    return totals


def combine_parts(first, second):
    peak = jnp.maximum(first[0], second[0])
    mass = first[1] * jnp.exp(first[0] - peak) + second[1] * jnp.exp(second[0] - peak)
    return (peak, mass, first[2] + second[2])


def shards(token_ids, embed_table, w_qkv, w_out, ln_gain, ln_bias, centroids_t, assignments):
    dp_size = lax.axis_size("dp")
    fsdp_size = lax.axis_size("fsdp")
    dp_rank = lax.axis_index("dp")
    fsdp_rank = lax.axis_index("fsdp")
    vocab_rows = embed_table.shape[0]
    local_ids = token_ids - fsdp_rank * vocab_rows
    inside = (local_ids >= 0) & (local_ids < vocab_rows)
    looked = jnp.take(embed_table, jnp.clip(local_ids, 0, vocab_rows - 1), axis=0)
    looked = jnp.where(inside[:, None], looked, jnp.zeros_like(looked))
    inputs = (
        lax.psum_scatter(looked, "fsdp", scatter_dimension=0, tiled=True)
        .astype(jnp.float32)
        .astype(jnp.bfloat16)
    )
    qkv_full, out_full, cent_full = (
        lax.all_gather(w_qkv, "fsdp", axis=0, tiled=True),
        lax.all_gather(w_out, "fsdp", axis=0, tiled=True),
        lax.all_gather(centroids_t, "fsdp", axis=0, tiled=True),
    )
    encoded = encode(inputs, qkv_full, out_full, ln_gain, ln_bias)
    own_rows = encoded.shape[0]
    width = encoded.shape[1]
    block_width = cent_full.shape[1]
    per_dev = block_width // fsdp_size
    slab = lax.all_gather(encoded, "dp", axis=0, tiled=True)
    slab_assign = lax.dynamic_index_in_dim(
        assignments.reshape(dp_size, fsdp_size, own_rows), fsdp_rank, 1, keepdims=False
    ).reshape(-1)
    owned = slab_assign - dp_rank * block_width
    slab_rows = slab.shape[0]
    step_rows = math.gcd(slab_rows, 512)
    columns = jnp.arange(block_width, dtype=jnp.int32)

    def body_visit(totals, pieces):
        block_rows, local = pieces
        logits = jnp.dot(block_rows, cent_full, preferred_element_type=jnp.float32)
        peak = jnp.max(logits, axis=1)
        mass = jnp.sum(jnp.exp(logits - peak[:, None]), axis=1)
        hits = local[:, None] == columns[None, :]
        picked = jnp.sum(jnp.where(hits, logits, 0.0), axis=1)
        return (totals, (peak, mass, picked))

    start = jnp.zeros((1,), jnp.float32)
    partial_value, stats = lax.scan(
        body_visit,
        start,
        (
            slab.reshape(slab_rows // step_rows, step_rows, width),
            owned.reshape(slab_rows // step_rows, step_rows),
        ),
    )
    peaks, masses, picks = (stats[0].reshape(-1), stats[1].reshape(-1), stats[2].reshape(-1))
    peaks, masses, picks = joined((peaks, masses, picks), "dp", combine_parts)
    peak_own = lax.dynamic_slice_in_dim(peaks, dp_rank * own_rows, own_rows)
    mass_own = lax.dynamic_slice_in_dim(masses, dp_rank * own_rows, own_rows)
    pick_own = lax.dynamic_slice_in_dim(picks, dp_rank * own_rows, own_rows)
    token_loss = jnp.log(mass_own) + peak_own - pick_own
    share = lax.all_to_all(encoded, "fsdp", split_axis=1, concat_axis=0, tiled=True)
    every_rows = lax.all_gather(share, "dp", axis=0, tiled=True)
    block_local = assignments - dp_rank * block_width
    partial_share = one_hot_sums(every_rows, block_local, block_width)
    totals = lax.all_to_all(partial_share, "fsdp", split_axis=0, concat_axis=1, tiled=True)
    base = dp_rank * block_width + fsdp_rank * per_dev
    targets = base + jnp.arange(per_dev, dtype=jnp.int32)
    counts = jnp.sum((assignments[:, None] == targets[None, :]).astype(jnp.int32), axis=0)
    previous = lax.dynamic_slice_in_dim(cent_full, fsdp_rank * per_dev, per_dev, 1).T.astype(
        jnp.float32
    )
    new_centroids = jnp.where(
        counts[:, None] > 0, totals / jnp.maximum(counts, 1)[:, None].astype(jnp.float32), previous
    )
    return (token_loss, new_centroids)


VMEM_LIMIT = 46 * 1024 * 1024
CUTS = 2
WHOLE_VMEM = pl.BlockSpec(memory_space=pltpu.VMEM)


class Place:
    def __init__(self, deep):
        self.deep = deep
        self.dp, self.fsdp = lax.axis_index("dp"), lax.axis_index("fsdp")
        self.x, self.c = self.dp // 2, self.dp % 2
        self.z, self.y = self.fsdp // 2, self.fsdp % 2

    def at(self, x=None, c=None, z=None, y=None):
        x, c = self.x if x is None else x, self.c if c is None else c
        z, y = self.z if z is None else z, self.y if y is None else y
        return {"dp": x * 2 + c, "fsdp": z * 2 + y}

    def greet(self):
        barrier = pltpu.get_barrier_semaphore()
        everyone = 8 * self.deep
        me = self.dp * 2 * self.deep + self.fsdp

        @pl.loop(1, everyone)
        def each(k):
            peer = (me + k) % everyone
            there = {"dp": peer // (2 * self.deep), "fsdp": peer % (2 * self.deep)}
            pl.semaphore_signal(barrier, inc=1, device_id=there, device_id_type=pl.DeviceIdType.MESH)

    def met(self):
        pl.semaphore_wait(pltpu.get_barrier_semaphore(), 8 * self.deep - 1)


class Sender:
    def __init__(self, sems):
        self.sems, self.used, self.sent = sems, 0, []

    def send(self, src, dst, recv_sem, peer, when=None):
        copy = pltpu.make_async_remote_copy(
            src_ref=src,
            dst_ref=dst,
            send_sem=self.sems.at[self.used],
            recv_sem=recv_sem,
            device_id=peer,
            device_id_type=pl.DeviceIdType.MESH,
        )
        self.used += 1
        self.sent.append((copy, when))
        guarded(when, copy.start)

    def arrived(self, dst, recv_sem, peer, when=None):
        copy = pltpu.make_async_remote_copy(
            src_ref=dst,
            dst_ref=dst,
            send_sem=self.sems.at[0],
            recv_sem=recv_sem,
            device_id=peer,
            device_id_type=pl.DeviceIdType.MESH,
        )
        guarded(when, copy.wait_recv)

    def drain(self):
        for copy, when in self.sent:
            guarded(when, copy.wait_send)


def guarded(when, action):
    if when is None:
        action()
    else:
        pl.when(when)(action)


def near_first(z, k, deep):
    below, above = z, deep - 1 - z
    both = jnp.minimum(below, above)
    swing = z - (k + 1) // 2 if k % 2 else z + k // 2
    far = jnp.where(above > below, z + k - both, z - k + both)
    return jnp.where(k <= 2 * both, swing, far)


def passage(x, quarters, gain, bias, w_ref):
    width = x.shape[1]

    def dense(rows, q):
        weights = w_ref[q].reshape(width, width)
        return jnp.dot(rows, weights, preferred_element_type=jnp.float32)

    query, key, value = (dense(x, q).astype(jnp.bfloat16) for q in quarters[:3])
    context = []
    for head in range(HEADS):
        at = slice(head * HEAD, (head + 1) * HEAD)
        scores = lax.dot_general(
            query[:, at], key[:, at], (((1,), (1,)), ((), ())), preferred_element_type=jnp.float32
        ) * (1.0 / math.sqrt(HEAD))
        weight = jnp.exp(scores - jnp.max(scores, axis=1, keepdims=True))
        probs = (weight / jnp.sum(weight, axis=1, keepdims=True)).astype(jnp.bfloat16)
        context.append(jnp.dot(probs, value[:, at], preferred_element_type=jnp.float32))
    context = jnp.concatenate(context, axis=1).astype(jnp.bfloat16)
    mixed = dense(context, quarters[3]) + x.astype(jnp.float32)
    return layer_norm(mixed, gain, bias).astype(jnp.bfloat16)


def step_kernel(
    deep,
    ids_hbm,
    table_hbm,
    qkv_hbm,
    out_w_hbm,
    gain_hbm,
    bias_hbm,
    cent_hbm,
    assign_hbm,
    loss_ref,
    new_ref,
    ids,
    table,
    gain,
    bias,
    assign,
    assign_plane,
    id_columns,
    rows,
    w,
    from_y,
    joined_y,
    from_mate,
    from_far,
    cent,
    old,
    mine,
    tokens,
    hot,
    counts,
    stat,
    got,
    load_sems,
    send_sems,
    y_sems,
    mate_sems,
    far_sems,
    w_sems,
    cent_sems,
    token_sems,
    stat_send,
    stat_recv,
):
    place = Place(deep)
    x, c, z, y = place.x, place.c, place.z, place.y
    own = place.fsdp
    parts = 2 * deep
    vocab_rows, width = table.shape
    own_rows = mine.shape[0]
    per_dev = new_ref.shape[0]
    blocks = 4 * parts
    own_block = (z * 4 + place.dp) * 2 + y
    quarter, across = x * 2 + c, (1 - x) * 2 + c
    partner, x_side, y_side = place.at(c=1 - c), place.at(x=1 - x), place.at(y=1 - y)
    up, down = place.at(z=jnp.minimum(z + 1, deep - 1)), place.at(z=jnp.maximum(z - 1, 0))
    outer = (z == 0) | (z == 3)
    inner = (z == 1) | (z == 2)
    mate_z = z + 1 - 2 * (z % 2)
    mate = place.at(z=mate_z)
    far = [3 - 3 * (z // 2), 2 - z // 2]
    dests = far + [mate_z, z]

    loads = [
        pltpu.make_async_copy(ids_hbm, ids, load_sems.at[0]),
        pltpu.make_async_copy(table_hbm, table, load_sems.at[1]),
    ]
    for q in range(4):
        part = qkv_hbm.at[:, pl.ds(q * width, width)] if q < 3 else out_w_hbm
        loads.append(pltpu.make_async_copy(part, w.at[q, own], load_sems.at[2 + q]))
    loads.append(pltpu.make_async_copy(gain_hbm, gain, load_sems.at[6]))
    loads.append(pltpu.make_async_copy(bias_hbm, bias, load_sems.at[7]))
    loads.append(pltpu.make_async_copy(assign_hbm, assign, load_sems.at[8]))
    loads.append(
        pltpu.make_async_copy(
            cent_hbm.at[:, pl.ds(pl.multiple_of(own * per_dev, 128), per_dev)], cent.at[own], load_sems.at[9]
        )
    )
    for load in loads:
        load.start()
    place.greet()
    loads[0].wait()
    columns = ids[...].T
    for k in range(parts):
        id_columns[k // 2, k % 2] = columns[:, k : k + 1]
    loads[1].wait()

    def look(y0):
        local = id_columns[:, y0].reshape(deep * own_rows, 1) - own * vocab_rows
        hot = local == lax.broadcasted_iota(jnp.int32, (deep * own_rows, vocab_rows), 1)
        found = jnp.dot(
            jnp.where(hot, 1.0, 0.0).astype(jnp.bfloat16), table[...], preferred_element_type=jnp.float32
        )
        rows[y0] = found.astype(jnp.bfloat16).reshape(deep, own_rows, width)

    base = (place.dp * parts + own) * per_dev
    centroid = lax.broadcasted_iota(jnp.int32, (per_dev, 2 * own_rows), 0) + base

    def prepare(z1):
        for i in range(4):
            assign_plane[z1, :, i * 2 * own_rows : (i + 1) * 2 * own_rows] = assign[i * deep + z1]

        @pl.loop(0, 4)
        def each(i):
            ones = jnp.where(centroid == assign[i * deep + z1], 1.0, 0.0)
            hot[z1, :, pl.ds(pl.multiple_of(i * 2 * own_rows, 128), 2 * own_rows)] = ones.astype(jnp.bfloat16)
            counts[...] += jnp.sum(ones, axis=1, keepdims=True)

    counts[...] = jnp.zeros_like(counts)
    look(1 - y)
    for load in loads[2:]:
        load.wait()
    place.met()
    out = Sender(send_sems)

    def send_rows(to):
        out.send(rows.at[1 - y, to], from_y.at[to], y_sems.at[to], y_side)

    def w_send(q, s, peer, when=None):
        out.send(w.at[q, s], w.at[q, s], w_sems.at[q, s], peer, when)

    def w_wait(q, s):
        out.arrived(w.at[q, s], w_sems.at[q, s], partner)

    def give(z0, y0, when=None):
        to = z0 * 2 + y0
        part = pl.ds(pl.multiple_of(to * per_dev, 128), per_dev)
        out.send(
            cent_hbm.at[:, part], cent.at[own], cent_sems.at[own], {"dp": place.dp, "fsdp": to}, when
        )

    w_send(quarter, own, up, z + 1 < deep)
    w_send(quarter, own, down, z > 0)
    send_rows(dests[0])
    send_rows(dests[1])
    w_send(quarter, own, y_side)
    send_rows(dests[2])
    send_rows(dests[3])
    give(mate_z, y)
    give(3 - z, y, inner)
    look(y)
    prepare(0)

    def w_column(k):
        z0 = near_first(z, k, deep)
        s = z0 * 2 + y
        w_wait(quarter, s)
        w_send(quarter, s, up, (z0 < z) & (z + 1 < deep))
        w_send(quarter, s, down, (z0 > z) & (z > 0))
        w_send(quarter, s, y_side)
        w_send(quarter, s, x_side)
        w_send(quarter, s, partner)

    def join(to):
        out.arrived(from_y.at[to], y_sems.at[to], y_side)
        joined_y[to] = from_y[to] + rows[y, to]

    def hand(to, when):
        out.send(joined_y.at[to], from_mate.at[to], mate_sems.at[to], mate, when)

    def mate_arrived(to, when):
        out.arrived(from_mate.at[to], mate_sems.at[to], mate, when)

    w_column(1)
    join(dests[0])
    hand(dests[0], outer)
    w_column(2)
    give(3 - z, 1 - y)
    join(dests[1])
    hand(dests[1], outer)

    def onward(to):
        mate_arrived(to, inner)

        @pl.when(inner)
        def add():
            joined_y[to] = joined_y[to] + from_mate[to]

        out.send(joined_y.at[to], from_far, far_sems.at[0], place.at(z=to), inner)

    onward(dests[0])
    w_column(3)
    join(dests[2])
    hand(dests[2], None)
    onward(dests[1])
    give((z + 2) % deep, y)
    give(3 - z, y, outer)
    join(dests[3])
    for k in range(deep):
        s = near_first(z, k, deep) * 2 + (1 - y)
        w_wait(quarter, s)
        w_send(quarter, s, x_side)
        w_send(quarter, s, partner)
    give((z + 2) % deep, 1 - y)
    give(mate_z, 1 - y)
    give(z, 1 - y)
    for k in range(1, deep):
        prepare(k)
    others = [near_first(z, k, deep) * 2 + y for k in range(1, deep)]
    others += [near_first(z, k, deep) * 2 + (1 - y) for k in range(deep)]
    for s in others:
        w_wait(across, s)
        w_send(across, s, partner)
    mate_arrived(z, None)
    out.arrived(from_far, far_sems.at[0], mate)
    total = joined_y[z] + from_mate[z] + from_far[...]
    for q in (x * 2 + (1 - c), (1 - x) * 2 + (1 - c)):
        for s in others:
            w_wait(q, s)
    mine[...] = passage(total, range(4), gain[...], bias[...], w)

    x_first = c == 1
    second_xy = (jnp.where(x_first, 1 - x, x), jnp.where(x_first, y, 1 - y))
    third_xy = (jnp.where(x_first, x, 1 - x), jnp.where(x_first, 1 - y, y))
    second = place.at(x=second_xy[0], y=second_xy[1])
    third = place.at(x=third_xy[0], y=third_xy[1])

    def number(x0, c0, z0, y0):
        return (z0 * 4 + x0 * 2 + c0) * 2 + y0

    cut_rows = own_rows // CUTS

    def push(b, h, peer, when=None, src=None):
        lines = pl.ds(h * cut_rows, cut_rows)
        there = tokens.at[b, lines]
        out.send(there if src is None else src.at[lines], there, token_sems.at[b, h], peer, when)

    def wait(b, h):
        out.arrived(tokens.at[b, pl.ds(h * cut_rows, cut_rows)], token_sems.at[b, h], partner)

    for h in range(CUTS):
        push(own_block, h, up, z + 1 < deep, mine)
        push(own_block, h, down, z > 0, mine)
        for peer in (second, third, partner):
            push(own_block, h, peer, None, mine)
    tokens[own_block] = mine[...]

    def add_up(k, part, of):
        z1 = near_first(z, k, deep)
        span = pl.ds(part * per_dev // of, per_dev // of)
        term = jnp.dot(
            hot[z1, span, :],
            tokens[pl.ds(z1 * 8, 8)].reshape(8 * own_rows, width),
            preferred_element_type=jnp.float32,
        )
        if k == 0:
            new_ref[span, :] = term
        else:
            new_ref[span, :] += term

    def scores(k):
        z1 = near_first(z, k, deep)
        plane = tokens[pl.ds(z1 * 8, 8)].reshape(8 * own_rows, width)
        chunk = math.gcd(per_dev, 256)
        target = assign_plane[z1] - base

        def logits_of(first):
            return lax.dot_general(
                old[first : first + chunk, :], plane, (((1,), (1,)), ((), ())), preferred_element_type=jnp.float32
            )

        line = lax.broadcasted_iota(jnp.int32, (chunk, 8 * own_rows), 0)
        later = logits_of(0)
        for first in range(0, per_dev, chunk):
            logits = later
            if first + chunk < per_dev:
                later = logits_of(first + chunk)
            top = jnp.max(logits, axis=0, keepdims=True)
            found = jnp.sum(jnp.where(line == target - first, logits, 0.0), axis=0, keepdims=True)
            if first == 0:
                peak, pick = top, found
                mass = jnp.sum(jnp.exp(logits - peak), axis=0, keepdims=True)
            else:
                higher = jnp.maximum(peak, top)
                mass = mass * jnp.exp(peak - higher) + jnp.sum(
                    jnp.exp(logits - higher), axis=0, keepdims=True
                )
                peak, pick = higher, pick + found
        for i in range(8):
            at = slice(i * own_rows, (i + 1) * own_rows)
            for n, row in enumerate((peak, mass, pick)):
                stat[z1 * 8 + i, pl.ds(n, 1), :] = row[:, at]

        @pl.loop(0, 8)
        def tell(i):
            b = z1 * 8 + i
            pl.when(b != own_block)(stat_copy(b).start)

    def stat_copy(b):
        return pltpu.make_async_remote_copy(
            src_ref=stat.at[b],
            dst_ref=got.at[own_block],
            send_sem=stat_send.at[0],
            recv_sem=stat_recv.at[0],
            device_id={"dp": b % 8 // 2, "fsdp": b // 8 * 2 + b % 2},
            device_id_type=pl.DeviceIdType.MESH,
        )

    def take_centroids():
        for k in range(1, parts):
            s = (own + k) % parts
            out.arrived(cent.at[s], cent_sems.at[s], partner)
        old[...] = cent[...].reshape(width, per_dev).T

    def onward_z(k):
        z0 = near_first(z, k, deep)
        b = number(x, c, z0, y)
        for h in range(CUTS):
            wait(b, h)
            push(b, h, up, (z0 < z) & (z + 1 < deep))
            push(b, h, down, (z0 > z) & (z > 0))
            push(b, h, second)
            push(b, h, third)
            push(b, h, partner)

    def onward_second(k):
        b = number(second_xy[0], c, near_first(z, k, deep), second_xy[1])
        for h in range(CUTS):
            wait(b, h)
            push(b, h, third)
            push(b, h, partner)

    def finish(k):
        z1 = near_first(z, k, deep)
        for xx, yy in (third_xy, (1 - x, 1 - y)):
            b = number(xx, c, z1, yy)
            for h in range(CUTS):
                wait(b, h)
                push(b, h, partner)

    def theirs(k):
        z1 = near_first(z, k, deep)
        for x0 in range(2):
            for y0 in range(2):
                for h in range(CUTS):
                    wait(number(x0, 1 - c, z1, y0), h)

    onward_z(1)
    onward_second(0)
    onward_z(2)
    onward_second(1)
    onward_z(3)
    finish(0)
    onward_second(2)
    finish(1)
    onward_second(3)
    theirs(0)
    take_centroids()
    add_up(0, 0, 1)
    scores(0)
    finish(2)
    theirs(1)
    add_up(1, 0, 1)
    scores(1)
    finish(3)
    theirs(2)
    scores(2)
    theirs(3)
    scores(3)
    add_up(2, 0, 1)
    add_up(3, 0, 1)

    many = counts[...]
    new_ref[...] = jnp.where(
        many > 0, new_ref[...] / jnp.maximum(many, 1.0), old[...].astype(jnp.float32)
    )
    own_stat = pltpu.make_async_copy(stat.at[own_block], got.at[own_block], stat_recv.at[0])
    own_stat.start()
    sent = stat.at[pl.ds(0, blocks - 1)]
    pltpu.make_async_copy(sent, sent, stat_send.at[0]).wait()
    pltpu.make_async_copy(got, got, stat_recv.at[0]).wait()
    peaks, masses, picks = (got[:, k, :] for k in range(3))
    top = jnp.max(peaks, axis=0, keepdims=True)
    mass = jnp.sum(masses * jnp.exp(peaks - top), axis=0, keepdims=True)
    loss_ref[...] = jnp.log(mass) + top - jnp.sum(picks, axis=0, keepdims=True)
    out.drain()


def token_shards(token_ids, embed_table, w_qkv, w_out, ln_gain, ln_bias, centroids_t, assignments):
    parts = lax.axis_size("fsdp")
    deep = parts // 2
    blocks = 4 * parts
    width = embed_table.shape[1]
    feats = w_qkv.shape[0]
    own_rows = token_ids.shape[0] // parts
    per_dev = centroids_t.shape[1] // parts
    half = jnp.bfloat16
    block = (own_rows, width)
    sems = pltpu.SemaphoreType.DMA
    in_hbm = pl.BlockSpec(memory_space=pltpu.HBM)
    loss, new = pl.pallas_call(
        functools.partial(step_kernel, deep),
        out_shape=(
            jax.ShapeDtypeStruct((1, own_rows), jnp.float32),
            jax.ShapeDtypeStruct((per_dev, width), jnp.float32),
        ),
        in_specs=[in_hbm] * 8,
        out_specs=(WHOLE_VMEM, WHOLE_VMEM),
        scratch_shapes=[
            pltpu.VMEM((parts, own_rows), jnp.int32),
            pltpu.VMEM(embed_table.shape, half),
            pltpu.VMEM((1, width), jnp.float32),
            pltpu.VMEM((1, width), jnp.float32),
            pltpu.VMEM((blocks // 2, 1, 2 * own_rows), jnp.int32),
            pltpu.VMEM((deep, 1, 8 * own_rows), jnp.int32),
            pltpu.VMEM((deep, 2, own_rows, 1), jnp.int32),
            pltpu.VMEM((2, deep, *block), half),
            pltpu.VMEM((4, parts, feats, width), half),
            pltpu.VMEM((deep, *block), half),
            pltpu.VMEM((deep, *block), half),
            pltpu.VMEM((deep, *block), half),
            pltpu.VMEM(block, half),
            pltpu.VMEM((parts, feats, per_dev), half),
            pltpu.VMEM((per_dev, width), half),
            pltpu.VMEM(block, half),
            pltpu.VMEM((blocks, *block), half),
            pltpu.VMEM((deep, per_dev, 8 * own_rows), half),
            pltpu.VMEM((per_dev, 1), jnp.float32),
            pltpu.VMEM((blocks, 8, own_rows), jnp.float32),
            pltpu.VMEM((blocks, 8, own_rows), jnp.float32),
            sems((10,)),
            sems((64 * deep,)),
            sems((deep,)),
            sems((deep,)),
            sems((1,)),
            sems((4, parts)),
            sems((parts,)),
            sems((blocks, CUTS)),
            sems((1,)),
            sems((1,)),
        ],
        compiler_params=pltpu.CompilerParams(
            collective_id=0, has_side_effects=True, vmem_limit_bytes=VMEM_LIMIT
        ),
        name="whole_step",
    )(
        *(
            pltpu.with_memory_space_constraint(array, pltpu.HBM)
            for array in (
                token_ids.reshape(parts, own_rows),
                embed_table,
                w_qkv,
                w_out,
                ln_gain.reshape(1, width),
                ln_bias.reshape(1, width),
                centroids_t,
                assignments.reshape(blocks // 2, 1, 2 * own_rows),
            )
        )
    )
    return loss.reshape(own_rows), new


def plan(mesh):
    dp_size, fsdp_size = mesh.shape["dp"], mesh.shape["fsdp"]

    def either(*args):
        few_tokens = args[7].shape[0] <= args[6].shape[1]
        paired = dp_size == 4 and fsdp_size == 8
        return token_shards(*args) if few_tokens and paired else shards(*args)

    return either


def solution(mesh):
    return jax.shard_map(
        plan(mesh),
        mesh=mesh,
        in_specs=(
            P("dp"),
            P("fsdp", None),
            P("fsdp", None),
            P("fsdp", None),
            P(),
            P(),
            P("fsdp", "dp"),
            P(),
        ),
        out_specs=(P(("dp", "fsdp")), P(("dp", "fsdp"), None)),
        check_vma=False,
    )
```

```python
import functools
import math

import jax
import jax.numpy as jnp
from jax import lax
from jax.experimental import pallas as pl
from jax.experimental.pallas import tpu as pltpu
from jax.sharding import PartitionSpec as P

HEADS = 12
HEAD = 64
SEQ = 128


def joined(shard, axis, combine):
    everything = jax.tree.map(lambda part: lax.all_gather(part, axis), shard)
    initial = jax.tree.map(lambda part: part[0], everything)

    def lap(k, so_far):
        return combine(so_far, jax.tree.map(lambda part: part[k], everything))

    return lax.fori_loop(1, lax.axis_size(axis), lap, initial)


def layer_norm(values, ln_gain, ln_bias):
    center = values - jnp.mean(values, axis=-1, keepdims=True)
    spread = jnp.mean(center * center, axis=-1, keepdims=True)
    return center * lax.rsqrt(spread + 1e-05) * ln_gain + ln_bias


def encode(inputs, qkv_full, out_full, ln_gain, ln_bias):
    passages = inputs.shape[0] // SEQ
    packed = jnp.dot(inputs, qkv_full, preferred_element_type=jnp.float32).astype(jnp.bfloat16)
    packed = packed.reshape(passages, SEQ, 3, HEADS, HEAD)
    scores = jnp.einsum(
        "bqhd,bkhd->bhqk", packed[:, :, 0], packed[:, :, 1], preferred_element_type=jnp.float32
    ) * (1.0 / math.sqrt(HEAD))
    probs = jax.nn.softmax(scores, axis=-1).astype(jnp.bfloat16)
    context = jnp.einsum(
        "bhqk,bkhd->bqhd", probs, packed[:, :, 2], preferred_element_type=jnp.float32
    )
    context = context.astype(jnp.bfloat16).reshape(inputs.shape[0], HEADS * HEAD)
    mixed = jnp.dot(context, out_full, preferred_element_type=jnp.float32) + inputs.astype(
        jnp.float32
    )
    return layer_norm(mixed, ln_gain, ln_bias).astype(jnp.bfloat16)


def one_hot_sums(rows, targets, width):
    count = rows.shape[0]
    step_rows = math.gcd(count, 512)
    columns = jnp.arange(width, dtype=jnp.int32)

    def one_visit(totals, pieces):
        block_rows, block_targets = pieces
        hits = (block_targets[:, None] == columns[None, :]).astype(jnp.bfloat16)
        return (
            totals
            + lax.dot_general(
                hits, block_rows, (((0,), (0,)), ((), ())), preferred_element_type=jnp.float32
            ),
            None,
        )

    start = jnp.zeros((width, rows.shape[1]), jnp.float32)
    totals, unused = lax.scan(
        one_visit,
        start,
        (
            rows.reshape(count // step_rows, step_rows, rows.shape[1]),
            targets.reshape(count // step_rows, step_rows),
        ),
    )
    return totals


def combine_parts(first, second):
    peak = jnp.maximum(first[0], second[0])
    mass = first[1] * jnp.exp(first[0] - peak) + second[1] * jnp.exp(second[0] - peak)
    return (peak, mass, first[2] + second[2])


def shards(token_ids, embed_table, w_qkv, w_out, ln_gain, ln_bias, centroids_t, assignments):
    dp_size = lax.axis_size("dp")
    fsdp_size = lax.axis_size("fsdp")
    dp_rank = lax.axis_index("dp")
    fsdp_rank = lax.axis_index("fsdp")
    vocab_rows = embed_table.shape[0]
    local_ids = token_ids - fsdp_rank * vocab_rows
    inside = (local_ids >= 0) & (local_ids < vocab_rows)
    looked = jnp.take(embed_table, jnp.clip(local_ids, 0, vocab_rows - 1), axis=0)
    looked = jnp.where(inside[:, None], looked, jnp.zeros_like(looked))
    inputs = (
        lax.psum_scatter(looked, "fsdp", scatter_dimension=0, tiled=True)
        .astype(jnp.float32)
        .astype(jnp.bfloat16)
    )
    qkv_full, out_full, cent_full = (
        lax.all_gather(w_qkv, "fsdp", axis=0, tiled=True),
        lax.all_gather(w_out, "fsdp", axis=0, tiled=True),
        lax.all_gather(centroids_t, "fsdp", axis=0, tiled=True),
    )
    encoded = encode(inputs, qkv_full, out_full, ln_gain, ln_bias)
    own_rows = encoded.shape[0]
    width = encoded.shape[1]
    block_width = cent_full.shape[1]
    per_dev = block_width // fsdp_size
    slab = lax.all_gather(encoded, "dp", axis=0, tiled=True)
    slab_assign = lax.dynamic_index_in_dim(
        assignments.reshape(dp_size, fsdp_size, own_rows), fsdp_rank, 1, keepdims=False
    ).reshape(-1)
    owned = slab_assign - dp_rank * block_width
    slab_rows = slab.shape[0]
    step_rows = math.gcd(slab_rows, 512)
    columns = jnp.arange(block_width, dtype=jnp.int32)

    def body_visit(totals, pieces):
        block_rows, local = pieces
        logits = jnp.dot(block_rows, cent_full, preferred_element_type=jnp.float32)
        peak = jnp.max(logits, axis=1)
        mass = jnp.sum(jnp.exp(logits - peak[:, None]), axis=1)
        hits = local[:, None] == columns[None, :]
        picked = jnp.sum(jnp.where(hits, logits, 0.0), axis=1)
        return (totals, (peak, mass, picked))

    start = jnp.zeros((1,), jnp.float32)
    partial_value, stats = lax.scan(
        body_visit,
        start,
        (
            slab.reshape(slab_rows // step_rows, step_rows, width),
            owned.reshape(slab_rows // step_rows, step_rows),
        ),
    )
    peaks, masses, picks = (stats[0].reshape(-1), stats[1].reshape(-1), stats[2].reshape(-1))
    peaks, masses, picks = joined((peaks, masses, picks), "dp", combine_parts)
    peak_own = lax.dynamic_slice_in_dim(peaks, dp_rank * own_rows, own_rows)
    mass_own = lax.dynamic_slice_in_dim(masses, dp_rank * own_rows, own_rows)
    pick_own = lax.dynamic_slice_in_dim(picks, dp_rank * own_rows, own_rows)
    token_loss = jnp.log(mass_own) + peak_own - pick_own
    share = lax.all_to_all(encoded, "fsdp", split_axis=1, concat_axis=0, tiled=True)
    every_rows = lax.all_gather(share, "dp", axis=0, tiled=True)
    block_local = assignments - dp_rank * block_width
    partial_share = one_hot_sums(every_rows, block_local, block_width)
    totals = lax.all_to_all(partial_share, "fsdp", split_axis=0, concat_axis=1, tiled=True)
    base = dp_rank * block_width + fsdp_rank * per_dev
    targets = base + jnp.arange(per_dev, dtype=jnp.int32)
    counts = jnp.sum((assignments[:, None] == targets[None, :]).astype(jnp.int32), axis=0)
    previous = lax.dynamic_slice_in_dim(cent_full, fsdp_rank * per_dev, per_dev, 1).T.astype(
        jnp.float32
    )
    new_centroids = jnp.where(
        counts[:, None] > 0, totals / jnp.maximum(counts, 1)[:, None].astype(jnp.float32), previous
    )
    return (token_loss, new_centroids)


VMEM_LIMIT = 46 * 1024 * 1024
CUTS = 2
WHOLE_VMEM = pl.BlockSpec(memory_space=pltpu.VMEM)


class Place:
    def __init__(self, deep):
        self.deep = deep
        self.dp, self.fsdp = lax.axis_index("dp"), lax.axis_index("fsdp")
        self.x, self.c = self.dp // 2, self.dp % 2
        self.z, self.y = self.fsdp // 2, self.fsdp % 2

    def at(self, x=None, c=None, z=None, y=None):
        x, c = self.x if x is None else x, self.c if c is None else c
        z, y = self.z if z is None else z, self.y if y is None else y
        return {"dp": x * 2 + c, "fsdp": z * 2 + y}

    def greet(self):
        barrier = pltpu.get_barrier_semaphore()
        everyone = 8 * self.deep
        me = self.dp * 2 * self.deep + self.fsdp

        @pl.loop(1, everyone)
        def each(k):
            peer = (me + k) % everyone
            there = {"dp": peer // (2 * self.deep), "fsdp": peer % (2 * self.deep)}
            pl.semaphore_signal(barrier, inc=1, device_id=there, device_id_type=pl.DeviceIdType.MESH)

    def met(self):
        pl.semaphore_wait(pltpu.get_barrier_semaphore(), 8 * self.deep - 1)


class Sender:
    def __init__(self, sems):
        self.sems, self.used, self.sent = sems, 0, []

    def send(self, src, dst, recv_sem, peer, when=None):
        copy = pltpu.make_async_remote_copy(
            src_ref=src,
            dst_ref=dst,
            send_sem=self.sems.at[self.used],
            recv_sem=recv_sem,
            device_id=peer,
            device_id_type=pl.DeviceIdType.MESH,
        )
        self.used += 1
        self.sent.append((copy, when))
        guarded(when, copy.start)

    def arrived(self, dst, recv_sem, peer, when=None):
        copy = pltpu.make_async_remote_copy(
            src_ref=dst,
            dst_ref=dst,
            send_sem=self.sems.at[0],
            recv_sem=recv_sem,
            device_id=peer,
            device_id_type=pl.DeviceIdType.MESH,
        )
        guarded(when, copy.wait_recv)

    def drain(self):
        for copy, when in self.sent:
            guarded(when, copy.wait_send)


def guarded(when, action):
    if when is None:
        action()
    else:
        pl.when(when)(action)


def near_first(z, k, deep):
    below, above = z, deep - 1 - z
    both = jnp.minimum(below, above)
    swing = z - (k + 1) // 2 if k % 2 else z + k // 2
    far = jnp.where(above > below, z + k - both, z - k + both)
    return jnp.where(k <= 2 * both, swing, far)


def passage(x, quarters, gain, bias, w_ref):
    width = x.shape[1]

    def dense(rows, q):
        weights = w_ref[q].reshape(width, width)
        return jnp.dot(rows, weights, preferred_element_type=jnp.float32)

    query, key, value = (dense(x, q).astype(jnp.bfloat16) for q in quarters[:3])
    context = []
    for head in range(HEADS):
        at = slice(head * HEAD, (head + 1) * HEAD)
        scores = lax.dot_general(
            query[:, at], key[:, at], (((1,), (1,)), ((), ())), preferred_element_type=jnp.float32
        ) * (1.0 / math.sqrt(HEAD))
        weight = jnp.exp(scores - jnp.max(scores, axis=1, keepdims=True))
        probs = (weight / jnp.sum(weight, axis=1, keepdims=True)).astype(jnp.bfloat16)
        context.append(jnp.dot(probs, value[:, at], preferred_element_type=jnp.float32))
    context = jnp.concatenate(context, axis=1).astype(jnp.bfloat16)
    mixed = dense(context, quarters[3]) + x.astype(jnp.float32)
    return layer_norm(mixed, gain, bias).astype(jnp.bfloat16)


def step_kernel(
    deep,
    ids_hbm,
    table_hbm,
    qkv_hbm,
    out_w_hbm,
    gain_hbm,
    bias_hbm,
    cent_hbm,
    assign_hbm,
    loss_ref,
    new_ref,
    ids,
    table,
    gain,
    bias,
    assign,
    assign_plane,
    id_columns,
    rows,
    w,
    from_y,
    joined_y,
    from_mate,
    from_far,
    cent,
    old,
    mine,
    tokens,
    hot,
    counts,
    stat,
    got,
    load_sems,
    send_sems,
    y_sems,
    mate_sems,
    far_sems,
    w_sems,
    cent_sems,
    token_sems,
    stat_send,
    stat_recv,
):
    place = Place(deep)
    x, c, z, y = place.x, place.c, place.z, place.y
    own = place.fsdp
    parts = 2 * deep
    vocab_rows, width = table.shape
    own_rows = mine.shape[0]
    per_dev = new_ref.shape[0]
    blocks = 4 * parts
    own_block = (z * 4 + place.dp) * 2 + y
    quarter, across = x * 2 + c, (1 - x) * 2 + c
    partner, x_side, y_side = place.at(c=1 - c), place.at(x=1 - x), place.at(y=1 - y)
    up, down = place.at(z=jnp.minimum(z + 1, deep - 1)), place.at(z=jnp.maximum(z - 1, 0))
    outer = (z == 0) | (z == 3)
    inner = (z == 1) | (z == 2)
    mate_z = z + 1 - 2 * (z % 2)
    mate = place.at(z=mate_z)
    far = [3 - 3 * (z // 2), 2 - z // 2]
    dests = far + [mate_z, z]

    loads = [
        pltpu.make_async_copy(ids_hbm, ids, load_sems.at[0]),
        pltpu.make_async_copy(table_hbm, table, load_sems.at[1]),
    ]
    for q in range(4):
        part = qkv_hbm.at[:, pl.ds(q * width, width)] if q < 3 else out_w_hbm
        loads.append(pltpu.make_async_copy(part, w.at[q, own], load_sems.at[2 + q]))
    loads.append(pltpu.make_async_copy(gain_hbm, gain, load_sems.at[6]))
    loads.append(pltpu.make_async_copy(bias_hbm, bias, load_sems.at[7]))
    loads.append(pltpu.make_async_copy(assign_hbm, assign, load_sems.at[8]))
    loads.append(
        pltpu.make_async_copy(
            cent_hbm.at[:, pl.ds(pl.multiple_of(own * per_dev, 128), per_dev)], cent.at[own], load_sems.at[9]
        )
    )
    for load in loads:
        load.start()
    place.greet()
    loads[0].wait()
    columns = ids[...].T
    for k in range(parts):
        id_columns[k // 2, k % 2] = columns[:, k : k + 1]
    loads[1].wait()

    def look(y0):
        local = id_columns[:, y0].reshape(deep * own_rows, 1) - own * vocab_rows
        hot = local == lax.broadcasted_iota(jnp.int32, (deep * own_rows, vocab_rows), 1)
        found = jnp.dot(
            jnp.where(hot, 1.0, 0.0).astype(jnp.bfloat16), table[...], preferred_element_type=jnp.float32
        )
        rows[y0] = found.astype(jnp.bfloat16).reshape(deep, own_rows, width)

    base = (place.dp * parts + own) * per_dev
    centroid = lax.broadcasted_iota(jnp.int32, (per_dev, 2 * own_rows), 0) + base

    def prepare(z1):
        for i in range(4):
            assign_plane[z1, :, i * 2 * own_rows : (i + 1) * 2 * own_rows] = assign[i * deep + z1]

        @pl.loop(0, 4)
        def each(i):
            ones = jnp.where(centroid == assign[i * deep + z1], 1.0, 0.0)
            hot[z1, :, pl.ds(pl.multiple_of(i * 2 * own_rows, 128), 2 * own_rows)] = ones.astype(jnp.bfloat16)
            counts[...] += jnp.sum(ones, axis=1, keepdims=True)

    counts[...] = jnp.zeros_like(counts)
    look(1 - y)
    for load in loads[2:]:
        load.wait()
    place.met()
    out = Sender(send_sems)

    def send_rows(to):
        out.send(rows.at[1 - y, to], from_y.at[to], y_sems.at[to], y_side)

    def w_send(q, s, peer, when=None):
        out.send(w.at[q, s], w.at[q, s], w_sems.at[q, s], peer, when)

    def w_wait(q, s):
        out.arrived(w.at[q, s], w_sems.at[q, s], partner)

    def give(z0, y0, when=None):
        to = z0 * 2 + y0
        part = pl.ds(pl.multiple_of(to * per_dev, 128), per_dev)
        out.send(
            cent_hbm.at[:, part], cent.at[own], cent_sems.at[own], {"dp": place.dp, "fsdp": to}, when
        )

    w_send(quarter, own, up, z + 1 < deep)
    w_send(quarter, own, down, z > 0)
    send_rows(dests[0])
    send_rows(dests[1])
    w_send(quarter, own, y_side)
    send_rows(dests[2])
    send_rows(dests[3])
    give(mate_z, y)
    give(3 - z, y, inner)
    look(y)

    def w_column(k):
        z0 = near_first(z, k, deep)
        s = z0 * 2 + y
        w_wait(quarter, s)
        w_send(quarter, s, up, (z0 < z) & (z + 1 < deep))
        w_send(quarter, s, down, (z0 > z) & (z > 0))
        w_send(quarter, s, y_side)
        w_send(quarter, s, x_side)
        w_send(quarter, s, partner)

    def join(to):
        out.arrived(from_y.at[to], y_sems.at[to], y_side)
        joined_y[to] = from_y[to] + rows[y, to]

    def hand(to, when):
        out.send(joined_y.at[to], from_mate.at[to], mate_sems.at[to], mate, when)

    def mate_arrived(to, when):
        out.arrived(from_mate.at[to], mate_sems.at[to], mate, when)

    w_column(1)
    join(dests[0])
    hand(dests[0], outer)
    w_column(2)
    give(3 - z, 1 - y)
    join(dests[1])
    hand(dests[1], outer)

    def onward(to):
        mate_arrived(to, inner)

        @pl.when(inner)
        def add():
            joined_y[to] = joined_y[to] + from_mate[to]

        out.send(joined_y.at[to], from_far, far_sems.at[0], place.at(z=to), inner)

    onward(dests[0])
    w_column(3)
    join(dests[2])
    hand(dests[2], None)
    onward(dests[1])
    give((z + 2) % deep, y)
    give(3 - z, y, outer)
    join(dests[3])
    for k in range(deep):
        s = near_first(z, k, deep) * 2 + (1 - y)
        w_wait(quarter, s)
        w_send(quarter, s, x_side)
        w_send(quarter, s, partner)
    give((z + 2) % deep, 1 - y)
    give(mate_z, 1 - y)
    give(z, 1 - y)
    for k in range(deep):
        prepare(k)
    others = [near_first(z, k, deep) * 2 + y for k in range(1, deep)]
    others += [near_first(z, k, deep) * 2 + (1 - y) for k in range(deep)]
    for s in others:
        w_wait(across, s)
        w_send(across, s, partner)
    mate_arrived(z, None)
    out.arrived(from_far, far_sems.at[0], mate)
    total = joined_y[z] + from_mate[z] + from_far[...]
    for q in (x * 2 + (1 - c), (1 - x) * 2 + (1 - c)):
        for s in others:
            w_wait(q, s)
    mine[...] = passage(total, range(4), gain[...], bias[...], w)

    x_first = c == 1
    second_xy = (jnp.where(x_first, 1 - x, x), jnp.where(x_first, y, 1 - y))
    third_xy = (jnp.where(x_first, x, 1 - x), jnp.where(x_first, 1 - y, y))
    second = place.at(x=second_xy[0], y=second_xy[1])
    third = place.at(x=third_xy[0], y=third_xy[1])

    def number(x0, c0, z0, y0):
        return (z0 * 4 + x0 * 2 + c0) * 2 + y0

    cut_rows = own_rows // CUTS

    def push(b, h, peer, when=None, src=None):
        lines = pl.ds(h * cut_rows, cut_rows)
        there = tokens.at[b, lines]
        out.send(there if src is None else src.at[lines], there, token_sems.at[b, h], peer, when)

    def wait(b, h):
        out.arrived(tokens.at[b, pl.ds(h * cut_rows, cut_rows)], token_sems.at[b, h], partner)

    for h in range(CUTS):
        push(own_block, h, up, z + 1 < deep, mine)
        push(own_block, h, down, z > 0, mine)
        for peer in (second, third, partner):
            push(own_block, h, peer, None, mine)
    tokens[own_block] = mine[...]

    def add_up(k, part, of):
        z1 = near_first(z, k, deep)
        span = pl.ds(part * per_dev // of, per_dev // of)
        term = jnp.dot(
            hot[z1, span, :],
            tokens[pl.ds(z1 * 8, 8)].reshape(8 * own_rows, width),
            preferred_element_type=jnp.float32,
        )
        if k == 0:
            new_ref[span, :] = term
        else:
            new_ref[span, :] += term

    def scores(k):
        z1 = near_first(z, k, deep)
        plane = tokens[pl.ds(z1 * 8, 8)].reshape(8 * own_rows, width)
        chunk = math.gcd(per_dev, 256)
        target = assign_plane[z1] - base

        def logits_of(first):
            return lax.dot_general(
                old[first : first + chunk, :], plane, (((1,), (1,)), ((), ())), preferred_element_type=jnp.float32
            )

        line = lax.broadcasted_iota(jnp.int32, (chunk, 8 * own_rows), 0)
        later = logits_of(0)
        for first in range(0, per_dev, chunk):
            logits = later
            if first + chunk < per_dev:
                later = logits_of(first + chunk)
            top = jnp.max(logits, axis=0, keepdims=True)
            found = jnp.sum(jnp.where(line == target - first, logits, 0.0), axis=0, keepdims=True)
            if first == 0:
                peak, pick = top, found
                mass = jnp.sum(jnp.exp(logits - peak), axis=0, keepdims=True)
            else:
                higher = jnp.maximum(peak, top)
                mass = mass * jnp.exp(peak - higher) + jnp.sum(
                    jnp.exp(logits - higher), axis=0, keepdims=True
                )
                peak, pick = higher, pick + found
        for i in range(8):
            at = slice(i * own_rows, (i + 1) * own_rows)
            for n, row in enumerate((peak, mass, pick)):
                stat[z1 * 8 + i, pl.ds(n, 1), :] = row[:, at]

        @pl.loop(0, 8)
        def tell(i):
            b = z1 * 8 + i
            pl.when(b != own_block)(stat_copy(b).start)

    def stat_copy(b):
        return pltpu.make_async_remote_copy(
            src_ref=stat.at[b],
            dst_ref=got.at[own_block],
            send_sem=stat_send.at[0],
            recv_sem=stat_recv.at[0],
            device_id={"dp": b % 8 // 2, "fsdp": b // 8 * 2 + b % 2},
            device_id_type=pl.DeviceIdType.MESH,
        )

    def take_centroids():
        for k in range(1, parts):
            s = (own + k) % parts
            out.arrived(cent.at[s], cent_sems.at[s], partner)
        old[...] = cent[...].reshape(width, per_dev).T

    def onward_z(k):
        z0 = near_first(z, k, deep)
        b = number(x, c, z0, y)
        for h in range(CUTS):
            wait(b, h)
            push(b, h, up, (z0 < z) & (z + 1 < deep))
            push(b, h, down, (z0 > z) & (z > 0))
            push(b, h, second)
            push(b, h, third)
            push(b, h, partner)

    def onward_second(k):
        b = number(second_xy[0], c, near_first(z, k, deep), second_xy[1])
        for h in range(CUTS):
            wait(b, h)
            push(b, h, third)
            push(b, h, partner)

    def finish(k):
        z1 = near_first(z, k, deep)
        for xx, yy in (third_xy, (1 - x, 1 - y)):
            b = number(xx, c, z1, yy)
            for h in range(CUTS):
                wait(b, h)
                push(b, h, partner)

    def theirs(k):
        z1 = near_first(z, k, deep)
        for x0 in range(2):
            for y0 in range(2):
                for h in range(CUTS):
                    wait(number(x0, 1 - c, z1, y0), h)

    onward_z(1)
    onward_second(0)
    onward_z(2)
    onward_second(1)
    onward_z(3)
    finish(0)
    onward_second(2)
    finish(1)
    onward_second(3)
    theirs(0)
    take_centroids()
    add_up(0, 0, 1)
    scores(0)
    finish(2)
    theirs(1)
    add_up(1, 0, 1)
    scores(1)
    finish(3)
    theirs(2)
    scores(2)
    theirs(3)
    scores(3)
    add_up(2, 0, 1)
    add_up(3, 0, 1)

    many = counts[...]
    new_ref[...] = jnp.where(
        many > 0, new_ref[...] / jnp.maximum(many, 1.0), old[...].astype(jnp.float32)
    )
    own_stat = pltpu.make_async_copy(stat.at[own_block], got.at[own_block], stat_recv.at[0])
    own_stat.start()
    sent = stat.at[pl.ds(0, blocks - 1)]
    pltpu.make_async_copy(sent, sent, stat_send.at[0]).wait()
    pltpu.make_async_copy(got, got, stat_recv.at[0]).wait()
    peaks, masses, picks = (got[:, k, :] for k in range(3))
    top = jnp.max(peaks, axis=0, keepdims=True)
    mass = jnp.sum(masses * jnp.exp(peaks - top), axis=0, keepdims=True)
    loss_ref[...] = jnp.log(mass) + top - jnp.sum(picks, axis=0, keepdims=True)
    out.drain()


def token_shards(token_ids, embed_table, w_qkv, w_out, ln_gain, ln_bias, centroids_t, assignments):
    parts = lax.axis_size("fsdp")
    deep = parts // 2
    blocks = 4 * parts
    width = embed_table.shape[1]
    feats = w_qkv.shape[0]
    own_rows = token_ids.shape[0] // parts
    per_dev = centroids_t.shape[1] // parts
    half = jnp.bfloat16
    block = (own_rows, width)
    sems = pltpu.SemaphoreType.DMA
    in_hbm = pl.BlockSpec(memory_space=pltpu.HBM)
    loss, new = pl.pallas_call(
        functools.partial(step_kernel, deep),
        out_shape=(
            jax.ShapeDtypeStruct((1, own_rows), jnp.float32),
            jax.ShapeDtypeStruct((per_dev, width), jnp.float32),
        ),
        in_specs=[in_hbm] * 8,
        out_specs=(WHOLE_VMEM, WHOLE_VMEM),
        scratch_shapes=[
            pltpu.VMEM((parts, own_rows), jnp.int32),
            pltpu.VMEM(embed_table.shape, half),
            pltpu.VMEM((1, width), jnp.float32),
            pltpu.VMEM((1, width), jnp.float32),
            pltpu.VMEM((blocks // 2, 1, 2 * own_rows), jnp.int32),
            pltpu.VMEM((deep, 1, 8 * own_rows), jnp.int32),
            pltpu.VMEM((deep, 2, own_rows, 1), jnp.int32),
            pltpu.VMEM((2, deep, *block), half),
            pltpu.VMEM((4, parts, feats, width), half),
            pltpu.VMEM((deep, *block), half),
            pltpu.VMEM((deep, *block), half),
            pltpu.VMEM((deep, *block), half),
            pltpu.VMEM(block, half),
            pltpu.VMEM((parts, feats, per_dev), half),
            pltpu.VMEM((per_dev, width), half),
            pltpu.VMEM(block, half),
            pltpu.VMEM((blocks, *block), half),
            pltpu.VMEM((deep, per_dev, 8 * own_rows), half),
            pltpu.VMEM((per_dev, 1), jnp.float32),
            pltpu.VMEM((blocks, 8, own_rows), jnp.float32),
            pltpu.VMEM((blocks, 8, own_rows), jnp.float32),
            sems((10,)),
            sems((64 * deep,)),
            sems((deep,)),
            sems((deep,)),
            sems((1,)),
            sems((4, parts)),
            sems((parts,)),
            sems((blocks, CUTS)),
            sems((1,)),
            sems((1,)),
        ],
        compiler_params=pltpu.CompilerParams(
            collective_id=0, has_side_effects=True, vmem_limit_bytes=VMEM_LIMIT
        ),
        name="whole_step",
    )(
        *(
            pltpu.with_memory_space_constraint(array, pltpu.HBM)
            for array in (
                token_ids.reshape(parts, own_rows),
                embed_table,
                w_qkv,
                w_out,
                ln_gain.reshape(1, width),
                ln_bias.reshape(1, width),
                centroids_t,
                assignments.reshape(blocks // 2, 1, 2 * own_rows),
            )
        )
    )
    return loss.reshape(own_rows), new


def plan(mesh):
    dp_size, fsdp_size = mesh.shape["dp"], mesh.shape["fsdp"]

    def either(*args):
        few_tokens = args[7].shape[0] <= args[6].shape[1]
        paired = dp_size == 4 and fsdp_size == 8
        return token_shards(*args) if few_tokens and paired else shards(*args)

    return either


def solution(mesh):
    return jax.shard_map(
        plan(mesh),
        mesh=mesh,
        in_specs=(
            P("dp"),
            P("fsdp", None),
            P("fsdp", None),
            P("fsdp", None),
            P(),
            P(),
            P("fsdp", "dp"),
            P(),
        ),
        out_specs=(P(("dp", "fsdp")), P(("dp", "fsdp"), None)),
        check_vma=False,
    )
```
